32 devices in a mesh: dp: 8 (over z, y), tensor: 4 (over x, core).
Axes of the slice: x: 2, y: 2, z: 4, core: 2. Of those that a mesh axis runs over, the one named last changes fastest.
Arguments:
- tokens: bfloat16 [16384, 768], P('dp'), may hold values from -6 to 6
- cotangent: bfloat16 [16384, 768], P('dp'), may hold values from -6 to 6
- key_lengths: int32 [32], P('dp'), may hold values from 256 to 512, as said below
- slot_counts: int32 [8], P('dp'), may hold values from 1 to 4, as said below
- w_query: bfloat16 [768, 768], P(None, 'tensor'), may hold values from -0.4375 to 0.4375
- b_query: bfloat16 [768], P('tensor'), may hold values from -3 to 3
- w_key: bfloat16 [768, 768], P(None, 'tensor'), may hold values from -0.21875 to 0.21875
- w_value: bfloat16 [768, 768], P(None, 'tensor'), may hold values from -0.21875 to 0.21875
- b_value: bfloat16 [768], P('tensor'), may hold values from -3 to 3
- w_out: bfloat16 [768, 768], P('tensor'), may hold values from -0.875 to 0.875
- b_out: bfloat16 [768], replicated, may hold values from -2 to 2
- attn_gain: bfloat16 [768], replicated, may hold values from 0.5 to 1.5
- attn_shift: bfloat16 [768], replicated, may hold values from -2 to 2
- w_up: bfloat16 [768, 3072], P(None, 'tensor'), may hold values from -0.21875 to 0.21875
- b_up: bfloat16 [3072], P('tensor'), may hold values from -3 to 3
- w_down: bfloat16 [3072, 768], P('tensor'), may hold values from -0.109375 to 0.109375
- b_down: bfloat16 [768], replicated, may hold values from -2 to 2
- ffn_gain: bfloat16 [768], replicated, may hold values from 0.5 to 1.5
- ffn_shift: bfloat16 [768], replicated, may hold values from -2 to 2
Outputs:
- layer_out: bfloat16 [16384, 768], P('dp')
- grad_tokens: bfloat16 [16384, 768], P('dp')
- grad_w_query: float32 [768, 768], P(None, 'tensor')
- grad_b_query: float32 [768], P('tensor')
- grad_w_key: float32 [768, 768], P(None, 'tensor')
- grad_w_value: float32 [768, 768], P(None, 'tensor')
- grad_b_value: float32 [768], P('tensor')
- grad_w_out: float32 [768, 768], P('tensor')
- grad_b_out: float32 [768], replicated
- grad_attn_gain: float32 [768], replicated
- grad_attn_shift: float32 [768], replicated
- grad_w_up: float32 [768, 3072], P(None, 'tensor')
- grad_b_up: float32 [3072], P('tensor')
- grad_w_down: float32 [3072, 768], P('tensor')
- grad_b_down: float32 [768], replicated
- grad_ffn_gain: float32 [768], replicated
- grad_ffn_shift: float32 [768], replicated
The draws below stay inside these ranges and needn't reach their ends.
Inputs may be any that keep to these rules, and one draw needn't show every extreme that they name: `key_lengths`: each slot's key length is between 256 and 512; the first slot's is 512. `slot_counts`: each group has 1 to 4 live slots; group 0 has 4.
All inputs are finite; a program needn't handle non-finite values.
Results may differ from the reference program's by a relative error of at most 0.019.
Values may be sent and summed in bfloat16 or wider, within the bound.
A program may use at most 128 MiB of HBM per device.

```python
import jax
import jax.numpy as jnp
from jax import lax

D = 768
HEADS = 12
HD = 64
FF = 3072
SEQ = 512
MB_MAX = 4
SLOTS = 32
TOKENS = 16384
N_DP = 8


def draw_key_lengths(key, part):
    drawn = jax.random.randint(key, (SLOTS,), SEQ // 2, SEQ + 1, dtype=jnp.int32)
    return drawn.at[0].set(SEQ)


def draw_slot_counts(key, part):
    drawn = jax.random.randint(key, (N_DP,), 1, MB_MAX + 1, dtype=jnp.int32)
    return drawn.at[0].set(MB_MAX)


def steps_of(key, extent, shards, low, high):
    def one(dim, blocks):
        heights = jax.random.uniform(jax.random.fold_in(jax.random.fold_in(key, 6), dim), (blocks,), jnp.float32, low / len(shards), high / len(shards))
        return jnp.repeat(jnp.exp(heights), extent[dim] // blocks).reshape((-1,) + (1,) * (len(extent) - dim - 1))

    loudness = one(*shards[0])
    for cut in shards[1:]:
        loudness = loudness * one(*cut)
    return loudness


def bell_draw(key, shape, spread, bound, shards=(), kind=jnp.bfloat16):
    factor_of = steps_of(key, shape, shards, -0.22, 0.18) if shards else 1.0
    result = jax.random.normal(key, shape, jnp.float32) * spread * factor_of
    return jnp.minimum(jnp.maximum(result, -bound), bound).astype(kind)


def setup_inputs(seed: int = 0) -> dict:
    streams_of = jax.random.split(jax.random.key(seed), 20)
    return {
        "tokens": bell_draw(streams_of[0], (TOKENS, D), 1.0, 6.0, ((0, 8),)),
        "cotangent": bell_draw(streams_of[1], (TOKENS, D), 1.0, 6.0, ((0, 8),)),
        "key_lengths": draw_key_lengths(jax.random.fold_in(streams_of[19], 71), 0),
        "slot_counts": draw_slot_counts(jax.random.fold_in(streams_of[19], 71), 0),
        "w_query": bell_draw(streams_of[4], (D, D), (D // 4) ** -0.5, 0.4375, ((1, 4),)),
        "b_query": bell_draw(streams_of[5], (D,), 0.5, 3.0, ((0, 4),)),
        "w_key": bell_draw(streams_of[6], (D, D), D ** -0.5, 0.21875, ((1, 4),)),
        "w_value": bell_draw(streams_of[7], (D, D), D ** -0.5, 0.21875, ((1, 4),)),
        "b_value": bell_draw(streams_of[8], (D,), 0.5, 3.0, ((0, 4),)),
        "w_out": bell_draw(streams_of[9], (D, D), (D // 16) ** -0.5, 0.875, ((0, 4),)),
        "b_out": bell_draw(streams_of[10], (D,), 0.3, 2.0),
        "attn_gain": jnp.clip(1.0 + 0.1 * jax.random.normal(streams_of[11], (D,), jnp.float32), 0.5, 1.5).astype(jnp.bfloat16),
        "attn_shift": bell_draw(streams_of[12], (D,), 0.3, 2.0),
        "w_up": bell_draw(streams_of[13], (D, FF), D ** -0.5, 0.21875, ((1, 4),)),
        "b_up": bell_draw(streams_of[14], (FF,), 0.5, 3.0, ((0, 4),)),
        "w_down": bell_draw(streams_of[15], (FF, D), FF ** -0.5, 0.109375, ((0, 4),)),
        "b_down": bell_draw(streams_of[16], (D,), 0.3, 2.0),
        "ffn_gain": jnp.clip(1.0 + 0.1 * jax.random.normal(streams_of[17], (D,), jnp.float32), 0.5, 1.5).astype(jnp.bfloat16),
        "ffn_shift": bell_draw(streams_of[18], (D,), 0.3, 2.0),
    }


@jax.custom_vjp
def low(v):
    return lax.optimization_barrier(v.astype(jnp.bfloat16)).astype(jnp.float32)

@jax.custom_vjp
def low_back(v):
    return v

def low_keep(v):
    return (low(v), None)

def low_pass(kept, grad):
    return (grad,)

def back_keep(v):
    return (v, None)

def back_low(kept, grad):
    return (low(grad),)
low.defvjp(low_keep, low_pass)
low_back.defvjp(back_keep, back_low)
HIGH = lax.Precision.HIGHEST

def matmul(left, right):
    return jnp.dot(left, right, precision=HIGH)

def layer_norm(hidden, gain, shift):
    center = hidden - lax.optimization_barrier(jnp.mean(hidden, -1, keepdims=True))
    variance = lax.optimization_barrier(jnp.mean(center * center, -1, keepdims=True))
    return center * lax.rsqrt(variance + 1e-05) * gain + shift

def attend(block):
    queries, key_rows, value_rows, length = block
    scores = jnp.einsum('qhd,khd->hqk', queries, key_rows, precision=HIGH) * 0.125
    scores = low_back(scores)
    valid = jnp.arange(SEQ) < length
    scores = jnp.where(valid[None, None, :], scores, -1e+30)
    attn_probs = low(jax.nn.softmax(scores, axis=-1))
    return jnp.einsum('hqk,khd->qhd', attn_probs, value_rows, precision=HIGH)

def forward(params, tokens, key_lengths, row_live):
    w_query, b_query, w_key, w_value, b_value, w_out, b_out, attn_gain, attn_shift, w_up, b_up, w_down, b_down, ffn_gain, ffn_shift = params
    queries = low(low_back(matmul(tokens, w_query) + b_query))
    key_rows = low(low_back(matmul(tokens, w_key)))
    value_rows = low(low_back(matmul(tokens, w_value) + b_value))
    head_shape = (SLOTS, SEQ, HEADS, HD)
    context = lax.map(jax.checkpoint(attend), (queries.reshape(head_shape), key_rows.reshape(head_shape), value_rows.reshape(head_shape), key_lengths))
    context = low(low_back(context.reshape(TOKENS, D)))
    attn_out = low_back(matmul(context, w_out) + b_out)
    first_out = layer_norm(tokens + attn_out, attn_gain, attn_shift)
    hidden_pre = low_back(matmul(low(first_out), w_up) + b_up)
    hidden_low = low(jax.nn.gelu(hidden_pre, approximate=False))
    ffn_out = low_back(matmul(hidden_low, w_down) + b_down)
    return layer_norm(first_out + ffn_out, ffn_gain, ffn_shift) * row_live[:, None]

def reference(tokens, cotangent, key_lengths, slot_counts, w_query, b_query, w_key, w_value, b_value, w_out, b_out, attn_gain, attn_shift, w_up, b_up, w_down, b_down, ffn_gain, ffn_shift):
    params = (w_query, b_query, w_key, w_value, b_value, w_out, b_out, attn_gain, attn_shift, w_up, b_up, w_down, b_down, ffn_gain, ffn_shift)
    params = tuple((weight.astype(jnp.float32) for weight in params))
    slot_ids = jnp.arange(SLOTS, dtype=jnp.int32)
    slot_live = slot_ids % MB_MAX < jnp.repeat(slot_counts, MB_MAX)
    row_live = jnp.repeat(slot_live, SEQ).astype(jnp.float32)

    def apply(weights, inputs):
        return forward(weights, inputs, key_lengths, row_live)
    layer_out, pullback = jax.vjp(apply, params, tokens.astype(jnp.float32))
    grads, grad_tokens = pullback(cotangent.astype(jnp.float32))
    return (layer_out.astype(jnp.bfloat16), grad_tokens.astype(jnp.bfloat16), grads[0], grads[1], grads[2], grads[3], grads[4], grads[5], grads[6], grads[7], grads[8], grads[9], grads[10], grads[11], grads[12], grads[13], grads[14])
```

```python
import jax
import jax.numpy as jnp
from jax import lax
from jax.sharding import PartitionSpec as P

HD = 64
SEQ = 512


def normalize(hidden, gain, shift):
    center = hidden - jnp.mean(hidden, -1, keepdims=True)
    inv_std = lax.rsqrt(jnp.mean(center * center, -1, keepdims=True) + 1e-05)
    normed = center * inv_std
    return (normed * gain + shift, normed, inv_std)


def norm_back(grad_normed, normed, inv_std):
    return inv_std * (
        grad_normed
        - jnp.mean(grad_normed, -1, keepdims=True)
        - normed * jnp.mean(grad_normed * normed, -1, keepdims=True)
    )


def gelu_exact(values):
    return jax.nn.gelu(values, approximate=False)


def column_sum(matrix):
    return jnp.sum(matrix.astype(jnp.float32), 0)


def run_slot(slot_index, live_factor, tokens, cotangent, key_lengths, params):
    (
        w_query,
        b_query,
        w_key,
        w_value,
        b_value,
        w_out,
        b_out,
        attn_gain,
        attn_shift,
        w_up,
        b_up,
        w_down,
        b_down,
        ffn_gain,
        ffn_shift,
    ) = params
    f32 = jnp.float32
    bf16 = jnp.bfloat16
    heads_local = w_query.shape[1] // HD
    head_shape = (SEQ, heads_local, HD)
    row_start = slot_index * SEQ
    tok_rows = lax.dynamic_slice_in_dim(tokens, row_start, SEQ, 0)
    grad_rows = lax.dynamic_slice_in_dim(cotangent, row_start, SEQ, 0).astype(f32) * live_factor
    length = key_lengths[slot_index]
    query_rows = (jnp.dot(tok_rows, w_query, preferred_element_type=f32) + b_query).astype(bf16)
    key_rows = jnp.dot(tok_rows, w_key, preferred_element_type=f32).astype(bf16)
    value_rows = (jnp.dot(tok_rows, w_value, preferred_element_type=f32) + b_value).astype(bf16)
    query_heads = query_rows.reshape(head_shape)
    key_heads = key_rows.reshape(head_shape)
    value_heads = value_rows.reshape(head_shape)
    valid_keys = (jnp.arange(SEQ) < length)[None, None, :]

    def masked_scores():
        scores = (
            jnp.einsum("qhd,khd->hqk", query_heads, key_heads, preferred_element_type=f32) * 0.125
        )
        return jnp.where(valid_keys, scores, -1e30)

    scores = masked_scores()
    top_score = jnp.max(scores, -1, keepdims=True)
    shifted_exp = jnp.exp(scores - top_score)
    totals = jnp.sum(shifted_exp, -1, keepdims=True)
    attn_probs = shifted_exp / totals
    log_total = top_score + jnp.log(totals)
    probs_low = attn_probs.astype(bf16)
    context = jnp.einsum("hqk,khd->qhd", probs_low, value_heads, preferred_element_type=f32)
    context = context.reshape(SEQ, -1).astype(bf16)
    attn_out = jnp.dot(context, w_out, preferred_element_type=f32) + b_out
    resid_one = tok_rows.astype(f32) + attn_out
    first_out, first_normed, first_inv = normalize(resid_one, attn_gain, attn_shift)
    first_low = first_out.astype(bf16)
    hidden_pre = jnp.dot(first_low, w_up, preferred_element_type=f32) + b_up
    hidden_act, gelu_pull = jax.vjp(gelu_exact, hidden_pre)
    hidden_low = hidden_act.astype(bf16)
    ffn_out = jnp.dot(hidden_low, w_down, preferred_element_type=f32) + b_down
    resid_two = first_out + ffn_out
    layer_rows, second_normed, second_inv = normalize(resid_two, ffn_gain, ffn_shift)
    grad_ffn_gain = jnp.sum(grad_rows * second_normed, 0)
    grad_ffn_shift = jnp.sum(grad_rows, 0)
    grad_resid_two = norm_back(grad_rows * ffn_gain, second_normed, second_inv)
    grad_ffn_low = grad_resid_two.astype(bf16)
    grad_b_down = column_sum(grad_ffn_low)
    grad_w_down = jnp.einsum("rf,rd->fd", hidden_low, grad_ffn_low, preferred_element_type=f32)
    grad_hidden = jnp.einsum("rd,fd->rf", grad_ffn_low, w_down, preferred_element_type=f32)
    grad_pre_low = gelu_pull(grad_hidden)[0].astype(bf16)
    grad_b_up = column_sum(grad_pre_low)
    grad_w_up = jnp.einsum("rd,rf->df", first_low, grad_pre_low, preferred_element_type=f32)
    up_back = jnp.einsum("rf,df->rd", grad_pre_low, w_up, preferred_element_type=f32)
    grad_first = grad_resid_two + up_back
    grad_attn_gain = jnp.sum(grad_first * first_normed, 0)
    grad_attn_shift = jnp.sum(grad_first, 0)
    grad_resid_one = norm_back(grad_first * attn_gain, first_normed, first_inv)
    grad_attn_low = grad_resid_one.astype(bf16)
    grad_b_out = column_sum(grad_attn_low)
    grad_w_out = jnp.einsum("rc,rd->cd", context, grad_attn_low, preferred_element_type=f32)
    grad_context = jnp.einsum("rd,cd->rc", grad_attn_low, w_out, preferred_element_type=f32)
    grad_context = grad_context.astype(bf16).reshape(head_shape)
    kept_probs = jnp.exp(masked_scores() - log_total)
    grad_probs = jnp.einsum("qhd,khd->hqk", grad_context, value_heads, preferred_element_type=f32)
    grad_scores = kept_probs * (grad_probs - jnp.sum(grad_probs * kept_probs, -1, keepdims=True))
    grad_scores = grad_scores.astype(bf16)
    grad_query = (
        jnp.einsum("hqk,khd->qhd", grad_scores, key_heads, preferred_element_type=f32) * 0.125
    )
    grad_query = grad_query.reshape(SEQ, -1).astype(bf16)
    grad_key = (
        jnp.einsum("hqk,qhd->khd", grad_scores, query_heads, preferred_element_type=f32) * 0.125
    )
    grad_key = grad_key.reshape(SEQ, -1).astype(bf16)
    grad_value = jnp.einsum(
        "hqk,qhd->khd", kept_probs.astype(bf16), grad_context, preferred_element_type=f32
    )
    grad_value = grad_value.reshape(SEQ, -1).astype(bf16)
    grad_b_query = column_sum(grad_query)
    grad_b_value = column_sum(grad_value)
    grad_w_query = jnp.einsum("rd,rc->dc", tok_rows, grad_query, preferred_element_type=f32)
    grad_w_key = jnp.einsum("rd,rc->dc", tok_rows, grad_key, preferred_element_type=f32)
    grad_w_value = jnp.einsum("rd,rc->dc", tok_rows, grad_value, preferred_element_type=f32)
    input_back = (
        jnp.einsum("rc,dc->rd", grad_query, w_query, preferred_element_type=f32)
        + jnp.einsum("rc,dc->rd", grad_key, w_key, preferred_element_type=f32)
        + jnp.einsum("rc,dc->rd", grad_value, w_value, preferred_element_type=f32)
    )
    grad_tok = grad_resid_one + input_back
    layer_low = (layer_rows * live_factor).astype(bf16)
    grad_low = grad_tok.astype(bf16)
    grads = (
        grad_w_query,
        grad_b_query,
        grad_w_key,
        grad_w_value,
        grad_b_value,
        grad_w_out,
        grad_b_out,
        grad_attn_gain,
        grad_attn_shift,
        grad_w_up,
        grad_b_up,
        grad_w_down,
        grad_b_down,
        grad_ffn_gain,
        grad_ffn_shift,
    )
    return (layer_low, grad_low, grads)


SPLIT = {0: 1, 1: 0, 2: 1, 3: 1, 4: 0, 5: 0, 9: 1, 10: 0, 11: 0}


def per_device(tokens, cotangent, key_lengths, slot_counts, *params):
    f32 = jnp.float32
    bf16 = jnp.bfloat16
    slot_index = lax.axis_index("tensor")
    full = tuple(
        lax.all_gather(p, "tensor", axis=SPLIT[i], tiled=True) if i in SPLIT else p
        for i, p in enumerate(params)
    )
    live_factor = (slot_index < slot_counts[0]).astype(f32)
    layer_low, grad_low, grads = run_slot(
        slot_index, live_factor, tokens, cotangent, key_lengths, full
    )
    layer_out = lax.all_gather(layer_low, "tensor", axis=0, tiled=True)
    grad_tokens = lax.all_gather(grad_low, "tensor", axis=0, tiled=True)
    outs = []
    for i, g in enumerate(grads):
        if g.ndim == 2:
            g = lax.psum_scatter(g.astype(bf16), "tensor", scatter_dimension=SPLIT[i], tiled=True)
            outs.append(lax.psum(g, "dp").astype(f32))
        elif i in SPLIT:
            g = lax.psum_scatter(g, "tensor", scatter_dimension=0, tiled=True)
            outs.append(lax.psum(g, "dp"))
        else:
            outs.append(lax.psum(g, ("dp", "tensor")))
    return (layer_out, grad_tokens, *outs)


def solution(mesh):
    placed = (
        P("dp", None),
        P("dp", None),
        P("dp"),
        P("dp"),
        P(None, "tensor"),
        P("tensor"),
        P(None, "tensor"),
        P(None, "tensor"),
        P("tensor"),
        P("tensor", None),
        P(),
        P(),
        P(),
        P(None, "tensor"),
        P("tensor"),
        P("tensor", None),
        P(),
        P(),
        P(),
    )
    return jax.shard_map(
        per_device,
        mesh=mesh,
        in_specs=placed,
        out_specs=(
            P("dp", None),
            P("dp", None),
            P(None, "tensor"),
            P("tensor"),
            P(None, "tensor"),
            P(None, "tensor"),
            P("tensor"),
            P("tensor", None),
            P(),
            P(),
            P(),
            P(None, "tensor"),
            P("tensor"),
            P("tensor", None),
            P(),
            P(),
            P(),
        ),
        check_vma=False,
    )
```

```python
import functools

import jax
import jax.numpy as jnp
from jax import lax
from jax.experimental import pallas as pl
from jax.experimental.pallas import tpu as pltpu
from jax.sharding import PartitionSpec as P

D = 768
HD = 64
SEQ = 512
MESH = pl.DeviceIdType.MESH
F32 = jnp.float32
BF16 = jnp.bfloat16
FF_PIECES = 6
PIECES = 10
LAG = {2: 1, 3: 3, 4: 4}


def flip(value, bit):
    return value + bit - 2 * bit * lax.rem(value // bit, 2)


def dot_nn(a, b):
    return lax.dot_general(a, b, (((1,), (0,)), ((), ())), preferred_element_type=F32)


def dot_nt(a, b):
    return lax.dot_general(a, b, (((1,), (1,)), ((), ())), preferred_element_type=F32)


def dot_tn(a, b):
    return lax.dot_general(a, b, (((0,), (0,)), ((), ())), preferred_element_type=F32)


def row_mean(value):
    return jnp.sum(value, -1, keepdims=True) * (1.0 / D)


def col_sum(value):
    return jnp.sum(value, 0, keepdims=True)


def norm_back(grad, normed, inv_std):
    return inv_std * (grad - row_mean(grad) - normed * row_mean(grad * normed))


def block(index, size):
    return pl.ds(pl.multiple_of(index * size, size), size)


def layer_kernel(dp_bits, tok_hbm, cot_hbm, len_ref, cnt_ref, qkv_own, out_own, up_own, down_own,
                 rows_ref, layer_out, grad_out, off_ref, oat_ref, vec_out,
                 wqkv, wo, wup, wdn, bias, tok, cot, qkv, ctx, lse, n1, r1, flow, hid, gd, gr2,
                 glow, acc, gctx, st, stage_rows, gff, r0, r1f, r2, r3, rx, rxa, vec_acc, vec_in,
                 ws, wr, gs, gr, vs, vr, os, orr, bs, br, ls, free_sem):
    t = lax.axis_index("tensor")
    d = lax.axis_index("dp")
    c = lax.rem(t, 2)
    x = t // 2
    b0 = lax.rem(d, 2)
    b1 = lax.rem(d // 2, 2)
    other = flip(t, 2)
    core = {"tensor": flip(t, 1)}
    across = {"tensor": other}
    dps = [{"dp": flip(d, 1 << k)} for k in range(dp_bits)]
    beside = dps[0]
    partners = (core, across, *dps)

    def send(src, dst, send_sem, recv_sem, device):
        return pltpu.make_async_remote_copy(
            src_ref=src, dst_ref=dst, send_sem=send_sem, recv_sem=recv_sem,
            device_id=device, device_id_type=MESH,
        )

    def slot_of(order):
        oc = lax.rem(order, 2)
        ox = order // 2
        return (x + ox - 2 * x * ox) * 2 + c + oc - 2 * c * oc

    loads = [
        pltpu.make_async_copy(tok_hbm.at[block(t, SEQ)], tok, ls.at[0]),
        pltpu.make_async_copy(qkv_own, wqkv.at[t], ls.at[1]),
        pltpu.make_async_copy(out_own, wo.at[t], ls.at[2]),
        pltpu.make_async_copy(up_own, wup.at[t], ls.at[3]),
        pltpu.make_async_copy(down_own, wdn.at[t], ls.at[4]),
        pltpu.make_async_copy(cot_hbm.at[block(t, SEQ)], cot, ls.at[5]),
    ]
    for load in loads:
        load.start()
    bias[t] = rows_ref[8:16]
    barrier = pltpu.get_barrier_semaphore()
    for device in partners:
        pl.semaphore_signal(barrier, inc=1, device_id=device, device_id_type=MESH)
    pl.semaphore_wait(barrier, len(partners))

    mine8 = rows_ref.at[pl.ds(8, 8)]
    bias_hop = send(mine8, bias.at[t], bs.at[0], br.at[0], across)
    bias_chip = send(mine8, bias.at[t], bs.at[1], br.at[1], core)
    bias_mate = send(bias.at[other], bias.at[other], bs.at[2], br.at[2], core)
    bias_hop.start()
    bias_chip.start()

    half_up = up_own.shape[0] // 2
    half_down = down_own.shape[0] // 2
    chunks = [
        (qkv_own, wqkv, 0, qkv_own.shape[0]), (out_own, wo, 0, out_own.shape[0]),
        (up_own, wup, 0, half_up), (up_own, wup, half_up, half_up),
        (down_own, wdn, 0, half_down), (down_own, wdn, half_down, half_down),
    ]

    def span(base, rows, which):
        return pl.ds(pl.multiple_of(base + which * (rows // 2), 16), rows // 2)

    hops, chips, relays, mates, lasts = [], [], [], [], []
    for i, (own, full, base, rows) in enumerate(chunks):
        hops.append(send(own.at[span(base, rows, b0)], full.at[t, span(base, rows, b0)],
                         ws.at[i, 1], wr.at[i, 1], across))
        chips.append(send(own.at[pl.ds(base, rows)], full.at[t, pl.ds(base, rows)],
                          ws.at[i, 0], wr.at[i, 0], core))
        here = full.at[other, span(base, rows, b0)]
        there = full.at[other, span(base, rows, 1 - b0)]
        relays.append(send(here, here, ws.at[i, 2], wr.at[i, 2], beside))
        mates.append(send(here, here, ws.at[i, 3], wr.at[i, 3], core))
        lasts.append(send(there, there, ws.at[i, 4], wr.at[i, 4], core))
        hops[i].start()
        chips[i].start()

    def from_across(i):
        hops[i].wait()
        relays[i].start()
        mates[i].start()

    def from_beside(i):
        relays[i].wait()
        lasts[i].start()

    def from_core(i):
        chips[i].wait()

    def from_far(i):
        mates[i].wait()
        lasts[i].wait()

    live = jnp.where(t < cnt_ref[0], 1.0, 0.0).astype(F32)
    length = len_ref[t]
    key_mask = jnp.where(
        lax.broadcasted_iota(jnp.int32, (1, SEQ), 1) < length, 0.0, -1e30
    ).astype(F32)
    vec_acc[0] = jnp.zeros_like(vec_acc[0])
    vec = vec_acc.at[0]

    def add_vec(row, value):
        vec[pl.ds(row, 1)] = vec[pl.ds(row, 1)] + value

    loads[0].wait()
    loads[1].wait()

    def attend(order, carry):
        s = slot_of(order)

        @pl.when(order == 1)
        def _():
            from_across(0)
            bias_hop.wait()
            bias_mate.start()
            from_core(0)
            bias_chip.wait()

        @pl.when(order == 2)
        def _():
            from_across(1)
            from_beside(0)
            bias_mate.wait()

        @pl.when(order == 3)
        def _():
            from_beside(1)
            from_far(0)

        for j in range(3):
            h = 3 * s + j
            w_rows = wqkv[s, 192 * j:192 * (j + 1)]
            qkv[h] = (dot_nt(tok[...], w_rows) + bias[s, 1 + j:2 + j, 0:192]).astype(BF16)
            keys = qkv[h, :, 64:128]
            values = qkv[h, :, 128:192]

            def rows(rb, carry):
                at = block(rb, 128)
                scores = dot_nt(qkv[h, at, 0:64], keys) * 0.125 + key_mask
                top = jnp.max(scores, -1, keepdims=True)
                expd = jnp.exp(scores - top)
                total = jnp.sum(expd, -1, keepdims=True)
                probs = (expd * (1.0 / total)).astype(BF16)
                ctx[s, at, 64 * j:64 * (j + 1)] = dot_nn(probs, values).astype(BF16)
                lane = lax.broadcasted_iota(jnp.int32, (128, 128), 1)
                lse[s, at] = jnp.where(lane == j, top + jnp.log(total), lse[s, at])
                return carry

            lax.fori_loop(0, SEQ // 128, rows, 0)
        return carry

    lse[...] = jnp.zeros_like(lse)
    lax.fori_loop(0, 4, attend, 0)

    from_across(2)
    from_core(1)
    from_far(1)
    loads[2].wait()
    gain1 = rows_ref[1:2]
    shift1 = rows_ref[2:3]

    def project(rb, carry):
        at = block(rb, 128)
        total = tok[at].astype(F32) + rows_ref[0:1]
        for s in range(4):
            total = total + dot_nn(ctx[s, at], wo[s])
        center = total - row_mean(total)
        inv = lax.rsqrt(row_mean(center * center) + 1e-5)
        normed = center * inv
        out = normed * gain1 + shift1
        n1[at] = normed
        r1[at] = inv
        flow[at] = out.astype(BF16)
        acc[at] = out + rows_ref[3:4]
        return carry

    lax.fori_loop(0, 4, project, 0)

    from_across(3)
    loads[3].wait()

    def raise_up(order, carry):
        s = slot_of(order)

        @pl.when(order == 1)
        def _():
            from_beside(2)
            from_core(2)
            from_core(3)

        @pl.when(order == 2)
        def _():
            from_across(4)
            from_beside(3)

        @pl.when(order == 3)
        def _():
            from_far(2)
            from_far(3)

        def rows(rb, carry):
            at = block(rb, 128)
            pre = dot_nn(flow[at], wup[s]) + bias[s, 0:1]
            cdf = 0.5 + 0.5 * lax.erf(pre * 0.7071067811865476)
            pdf = jnp.exp(pre * pre * -0.5) * 0.3989422804014327
            hid[s, at] = (pre * cdf).astype(BF16)
            gd[s, at] = (cdf + pre * pdf).astype(BF16)
            return carry

        lax.fori_loop(0, 4, rows, 0)
        return carry

    lax.fori_loop(0, 4, raise_up, 0)
    from_across(5)
    from_beside(4)
    loads[4].wait()

    def bring_down(order, carry):
        s = slot_of(order)

        @pl.when(order == 1)
        def _():
            from_core(4)
            from_core(5)

        @pl.when(order == 2)
        def _():
            from_beside(5)

        @pl.when(order == 3)
        def _():
            from_far(4)
            from_far(5)

        def rows(rb, carry):
            at = block(rb, 256)
            acc[at] = acc[at] + dot_nn(hid[s, at], wdn[s])
            return carry

        lax.fori_loop(0, 2, rows, 0)
        return carry

    lax.fori_loop(0, 4, bring_down, 0)

    loads[5].wait()
    gain2 = rows_ref[4:5]
    shift2 = rows_ref[5:6]
    lay = stage_rows.at[0]
    gtok = stage_rows.at[1]

    def second(rb, carry):
        at = block(rb, 128)
        total = acc[at]
        center = total - row_mean(total)
        inv = lax.rsqrt(row_mean(center * center) + 1e-5)
        normed = center * inv
        lay[at] = (live * (normed * gain2 + shift2)).astype(BF16)
        grad = live * cot[at].astype(F32)
        add_vec(1, col_sum(grad * normed))
        add_vec(2, col_sum(grad))
        back = norm_back(grad * gain2, normed, inv)
        low = back.astype(BF16)
        gr2[at] = back
        glow[at] = low
        add_vec(0, col_sum(low.astype(F32)))
        acc[at] = jnp.zeros_like(total)
        return carry

    lax.fori_loop(0, 4, second, 0)

    def spread(i, src, dst):
        return (
            pltpu.make_async_copy(src, dst.at[t], ls.at[6 + i]),
            send(src, dst.at[t], os.at[i, 0], orr.at[i, 0], across),
            send(src, dst.at[t], os.at[i, 1], orr.at[i, 1], core),
            send(dst.at[other], dst.at[other], os.at[i, 2], orr.at[i, 2], core),
        )

    lay_copies = spread(0, lay, layer_out)
    for copy in lay_copies[:3]:
        copy.start()

    n_exchange = dp_bits - 2
    last = 4 + n_exchange + 2
    lag = dict(LAG)
    for s in range(5, last + 1):
        lag[s] = lag[s - 1] + (2 if s == last else 1)

    def att_rows(shard, quarter, count):
        return pl.ds(pl.multiple_of((shard * 4 + quarter) * 48, 48), count)

    def views(ff, p):
        out = off_ref if ff else oat_ref
        if ff:
            return dict(
                s0=gff.at[p, 1 - c], k0=gff.at[p, c], r0=r0.at[p],
                s1=gff.at[p, c, 1 - x], k1=gff.at[p, c, x], r1=r1f.at[p],
                s2=gff.at[p, c, x, 1 - b0], k2=gff.at[p, c, x, b0], r2=r2.at[p],
                s3=gff.at[p, c, x, b0, 1 - b1], k3=gff.at[p, c, x, b0, b1], r3=r3.at[p],
                rx=rx, o1=out.at[p, b0, b1], o0=out.at[p, b0],
            )
        g = wdn.at[p]
        r = wup.at[p]
        me = 2 * c + x
        return dict(
            s0=g.at[att_rows(2 * (1 - c), 0, 384)], k0=g.at[att_rows(2 * c, 0, 384)],
            r0=r.at[pl.ds(0, 384)],
            s1=g.at[att_rows(2 * c + 1 - x, 0, 192)], k1=g.at[att_rows(me, 0, 192)],
            r1=r.at[pl.ds(384, 192)],
            s2=g.at[att_rows(me, 2 * (1 - b0), 96)], k2=g.at[att_rows(me, 2 * b0, 96)],
            r2=r.at[pl.ds(576, 96)],
            s3=g.at[att_rows(me, 2 * b0 + 1 - b1, 48)], k3=g.at[att_rows(me, 2 * b0 + b1, 48)],
            r3=r.at[pl.ds(672, 48)],
            rx=rxa, o1=out.at[p, b0, b1], o0=out.at[p, b0],
        )

    def stage_copy(s, p, ff):
        v = views(ff, p)
        base = 0 if ff else FF_PIECES
        sems = (gs.at[s, base + p], gr.at[s, base + p])
        if s < 4:
            return send(v[f"s{s}"], v[f"r{s}"], *sems, (core, across, dps[0], dps[1])[s])
        if s < 4 + n_exchange:
            k = s - 4
            return send(v["k3"], v["rx"].at[p, k], *sems, dps[2 + k])
        if s == 4 + n_exchange:
            return send(v["o1"], v["o1"], *sems, dps[1])
        return send(v["o0"], v["o0"], *sems, dps[0])

    def combine(s, p, ff):
        v = views(ff, p)
        if s < 4:
            keep, got = v[f"k{s}"], v[f"r{s}"]
            keep[...] = keep[...] + got[...]
        elif s < 4 + n_exchange:
            k = s - 4
            total = v["k3"][...] + v["rx"].at[p, k][...]
            v["o1" if k == n_exchange - 1 else "k3"][...] = total

    def run_stage(s, p, ff):
        if s > 0:
            stage_copy(s - 1, p, ff).wait()
            combine(s - 1, p, ff)
        if s < last:
            stage_copy(s, p, ff).start()

    def down_grad(i, carry):
        def shard(s, carry):
            value = dot_tn(hid[s, :, block(i, 256)], glow[...]).astype(BF16)
            for q in range(4):
                gff[i, lax.rem(s, 2), s // 2, q // 2, q % 2] = value[64 * q:64 * (q + 1)]
            return carry

        lax.fori_loop(0, 4, shard, 0)
        run_stage(0, i, True)

        @pl.when(i > 0)
        def _():
            run_stage(1, i - 1, True)

        return carry

    lax.fori_loop(0, 3, down_grad, 0)

    def ffn_back(s, carry):
        @pl.when(s == 1)
        def _():
            run_stage(1, 2, True)
            lay_copies[1].wait()
            lay_copies[3].start()

        def rows(rb, carry):
            at = block(rb, 256)
            low = (dot_nt(glow[at], wdn[s]) * gd[s, at].astype(F32)).astype(BF16)
            gd[s, at] = low
            add_vec(8 + s, col_sum(low.astype(F32)))
            acc[at] = acc[at] + dot_nt(low, wup[s])
            return carry

        lax.fori_loop(0, 2, rows, 0)
        return carry

    lax.fori_loop(0, 4, ffn_back, 0)
    for device in partners:
        pl.semaphore_signal(free_sem, inc=1, device_id=device, device_id_type=MESH)

    def up_grad(i, carry):
        def shard(s, carry):
            value = dot_tn(flow[:, block(i, 256)], gd[s]).astype(BF16)
            for q in range(4):
                gff[3 + i, lax.rem(s, 2), s // 2, q // 2, q % 2] = value[64 * q:64 * (q + 1)]
            return carry

        lax.fori_loop(0, 4, shard, 0)
        run_stage(0, 3 + i, True)

        @pl.when(i > 0)
        def _():
            run_stage(1, 2 + i, True)

        return carry

    lax.fori_loop(0, 3, up_grad, 0)

    def first_back(rb, carry):
        at = block(rb, 128)
        grad = gr2[at] + acc[at]
        normed = n1[at]
        add_vec(4, col_sum(grad * normed))
        add_vec(5, col_sum(grad))
        back = norm_back(grad * gain1, normed, r1[at])
        low = back.astype(BF16)
        acc[at] = back
        glow[at] = low
        add_vec(3, col_sum(low.astype(F32)))
        return carry

    lax.fori_loop(0, 4, first_back, 0)
    run_stage(1, 5, True)

    pl.semaphore_wait(free_sem, len(partners))

    def out_back(s, carry):
        home = att_rows(2 * lax.rem(s, 2) + s // 2, 0, 192)
        wdn[0, home] = dot_tn(ctx[s], glow[...]).astype(BF16)
        back = dot_nt(glow[...], wo[s]).astype(BF16)
        for j in range(3):
            gctx[3 * s + j] = back[:, 64 * j:64 * (j + 1)]
        return carry

    lax.fori_loop(0, 4, out_back, 0)
    run_stage(0, 0, False)

    def tail_stages(n):
        for s in range(last, 1, -1):
            for ff in (True, False):
                p = (n - lag[s]) // 3
                low, high = (0, FF_PIECES) if ff else (FF_PIECES, PIECES)

                @pl.when((n >= lag[s]) & (lax.rem(n + 300 - lag[s], 3) == 0) & (p >= low) & (p < high))
                def _():
                    run_stage(s, p - low, ff)

    def head_back(n, carry):
        s = slot_of(lax.rem(n, 4))
        j = n // 4
        h = 3 * s + j
        keys = qkv[h, :, 64:128]
        values = qkv[h, :, 128:192]
        keys_t = keys.T
        st[...] = jnp.zeros_like(st)

        def rows(rb, carry):
            at = block(rb, 128)
            query = qkv[h, at, 0:64]
            gout = gctx[h, at]
            lane = lax.broadcasted_iota(jnp.int32, (128, 128), 1)
            norm = jnp.sum(jnp.where(lane == j, lse[s, at], 0.0), -1, keepdims=True)
            probs = jnp.exp(dot_nt(query, keys) * 0.125 + key_mask - norm)
            gprobs = dot_nt(gout, values)
            scored = probs * (gprobs - jnp.sum(gprobs * probs, -1, keepdims=True))
            scored = scored.astype(BF16)
            st[0:64, at] = dot_nt(keys_t, scored)
            st[64:128] = st[64:128] + dot_tn(query, scored)
            st[128:192] = st[128:192] + dot_tn(gout, probs.astype(BF16))
            return carry

        lax.fori_loop(0, SEQ // 128, rows, 0)
        row = lax.broadcasted_iota(jnp.int32, (192, 1), 0)
        packed = (st[...] * jnp.where(row < 128, 0.125, 1.0)).astype(BF16)
        home = att_rows(2 * lax.rem(s, 2) + s // 2, 0, 192)
        wdn[1 + j, home] = dot_nn(packed, tok[...]).astype(BF16)
        sums = dot_nt(jnp.ones((8, SEQ), BF16), packed)
        vec[pl.ds(12 + h, 1), 0:192] = sums[0:1]
        w_rows = wqkv[s, block(j, 192)]

        acc[...] = acc[...] + dot_tn(packed, w_rows)

        @pl.when(n == 0)
        def _():
            run_stage(1, 0, False)

        @pl.when(lax.rem(n, 4) == 3)
        def _():
            run_stage(0, 1 + j, False)

        @pl.when((n > 0) & (lax.rem(n, 4) == 0))
        def _():
            run_stage(1, j, False)

        tail_stages(n)
        return carry

    lax.fori_loop(0, 12, head_back, 0)
    gtok[...] = acc[...].astype(BF16)
    tok_copies = spread(1, gtok, grad_out)
    for copy in tok_copies[:3]:
        copy.start()

    def vec_copy(k):
        return send(vec_acc.at[k], vec_in.at[k], vs.at[k], vr.at[k], partners[k])

    vec_copy(0).start()
    run_stage(1, 3, False)
    end = max(3 * (PIECES - 1) + lag[last], 13 + 2 * len(partners))

    def drain(n, carry):
        tail_stages(n)
        for k in range(len(partners)):
            @pl.when(n == 14 + 2 * k)
            def _():
                vec_copy(k).wait()
                total = vec_acc[k] + vec_in[k]
                if k == len(partners) - 1:
                    vec_out[...] = total
                else:
                    vec_acc[k + 1] = total
                    vec_copy(k + 1).start()

        @pl.when(n == 30)
        def _():
            tok_copies[1].wait()
            tok_copies[3].start()

        return carry

    lax.fori_loop(12, end + 1, drain, 0)
    for copies in (lay_copies, tok_copies):
        copies[0].wait()
        copies[2].wait()
        copies[3].wait()


def run_layer(dp, tokens, cotangent, key_lengths, slot_counts, shards, rows):
    dp_bits = dp.bit_length() - 1
    n_exchange = dp_bits - 2
    stages = 4 + n_exchange + 2
    links = dp_bits + 2
    vmem = pl.BlockSpec(memory_space=pltpu.VMEM)
    smem = pl.BlockSpec(memory_space=pltpu.SMEM)
    hbm = pl.BlockSpec(memory_space=pltpu.HBM)
    dma = pltpu.SemaphoreType.DMA
    return pl.pallas_call(
        functools.partial(layer_kernel, dp_bits),
        out_shape=[
            jax.ShapeDtypeStruct((4, SEQ, D), BF16),
            jax.ShapeDtypeStruct((4, SEQ, D), BF16),
            jax.ShapeDtypeStruct((6, 2, 2, 64, D), BF16),
            jax.ShapeDtypeStruct((4, 2, 2, 48, D), BF16),
            jax.ShapeDtypeStruct((24, D), F32),
        ],
        in_specs=[hbm, hbm, smem, smem] + [hbm] * 4 + [vmem],
        out_specs=[hbm] * 2 + [vmem] * 3,
        scratch_shapes=[
            *[pltpu.VMEM((4, *s.shape), BF16) for s in shards],
            pltpu.VMEM((4, 8, D), F32),
            pltpu.VMEM((SEQ, D), BF16),
            pltpu.VMEM((SEQ, D), BF16),
            pltpu.VMEM((12, SEQ, 192), BF16),
            pltpu.VMEM((4, SEQ, 192), BF16),
            pltpu.VMEM((4, SEQ, 128), F32),
            pltpu.VMEM((SEQ, D), F32),
            pltpu.VMEM((SEQ, 1), F32),
            pltpu.VMEM((SEQ, D), BF16),
            pltpu.VMEM((4, SEQ, D), BF16),
            pltpu.VMEM((4, SEQ, D), BF16),
            pltpu.VMEM((SEQ, D), F32),
            pltpu.VMEM((SEQ, D), BF16),
            pltpu.VMEM((SEQ, D), F32),
            pltpu.VMEM((12, SEQ, 64), BF16),
            pltpu.VMEM((192, SEQ), F32),
            pltpu.VMEM((2, SEQ, D), BF16),
            pltpu.VMEM((6, 2, 2, 2, 2, 64, D), BF16),
            pltpu.VMEM((6, 2, 2, 2, 64, D), BF16),
            pltpu.VMEM((6, 2, 2, 64, D), BF16),
            pltpu.VMEM((6, 2, 64, D), BF16),
            pltpu.VMEM((6, 64, D), BF16),
            pltpu.VMEM((6, n_exchange, 64, D), BF16),
            pltpu.VMEM((4, n_exchange, 48, D), BF16),
            pltpu.VMEM((links, 24, D), F32),
            pltpu.VMEM((links, 24, D), F32),
            dma((6, 5)), dma((6, 5)),
            dma((stages, PIECES)), dma((stages, PIECES)),
            dma((links,)), dma((links,)),
            dma((2, 3)), dma((2, 3)),
            dma((3,)), dma((3,)),
            dma((8,)),
            pltpu.SemaphoreType.REGULAR,
        ],
        compiler_params=pltpu.CompilerParams(
            collective_id=0, has_side_effects=True, vmem_limit_bytes=67043328
        ),
    )(tokens, cotangent, key_lengths, slot_counts, *shards, rows)


def per_device(dp, tokens, cotangent, key_lengths, slot_counts, *params):
    (w_query, b_query, w_key, w_value, b_value, w_out, b_out, attn_gain, attn_shift,
     w_up, b_up, w_down, b_down, ffn_gain, ffn_shift) = params
    slot = lax.axis_index("tensor")
    heads = w_query.shape[1] // HD
    qkv = jnp.stack([w.reshape(D, heads, HD) for w in (w_query, w_key, w_value)], 1)
    qkv = qkv.transpose(2, 1, 3, 0).reshape(-1, D)
    q_bias = b_query.reshape(heads, HD)
    v_bias = b_value.reshape(heads, HD)
    qkv_bias = jnp.concatenate(
        (q_bias, jnp.zeros_like(q_bias), v_bias, jnp.zeros((heads, D - 3 * HD), BF16)), 1
    )
    rows = jnp.concatenate(
        [v[None] for v in (b_out, attn_gain, attn_shift, b_down, ffn_gain, ffn_shift)]
        + [jnp.zeros((2, D), BF16), b_up[None], qkv_bias, jnp.zeros((4, D), BF16)], 0
    ).astype(F32)
    layer, grad, off, oat, vec = run_layer(
        dp, tokens, cotangent, key_lengths, slot_counts, (qkv, w_out, w_up, w_down), rows
    )
    off = off.reshape(2, -1, D).astype(F32)
    oat = oat.reshape(4, -1, D)
    g_out = oat[0].astype(F32)
    g_qkv = oat[1:].reshape(heads, 3, HD, D)
    g_q, g_k, g_v = (g_qkv[:, i].reshape(-1, D).T.astype(F32) for i in range(3))
    b_qkv = lax.dynamic_slice_in_dim(vec[12:, :3 * HD], slot * heads, heads)
    gb_up = lax.dynamic_slice_in_dim(vec[8:12], slot, 1)[0]
    return (layer.reshape(-1, D), grad.reshape(-1, D),
            g_q, b_qkv[:, :HD].reshape(-1), g_k, g_v, b_qkv[:, 2 * HD:].reshape(-1), g_out,
            vec[3], vec[4], vec[5], off[1], gb_up, off[0], vec[0], vec[1], vec[2])


def solution(mesh):
    placed = (
        P("dp", None),
        P("dp", None),
        P("dp"),
        P("dp"),
        P(None, "tensor"),
        P("tensor"),
        P(None, "tensor"),
        P(None, "tensor"),
        P("tensor"),
        P("tensor", None),
        P(),
        P(),
        P(),
        P(None, "tensor"),
        P("tensor"),
        P("tensor", None),
        P(),
        P(),
        P(),
    )
    return jax.shard_map(
        functools.partial(per_device, mesh.shape["dp"]),
        mesh=mesh,
        in_specs=placed,
        out_specs=(
            P("dp", None),
            P("dp", None),
            P(None, "tensor"),
            P("tensor"),
            P(None, "tensor"),
            P(None, "tensor"),
            P("tensor"),
            P("tensor", None),
            P(),
            P(),
            P(),
            P(None, "tensor"),
            P("tensor"),
            P("tensor", None),
            P(),
            P(),
            P(),
        ),
        check_vma=False,
    )
```

```python
import functools

import jax
import jax.numpy as jnp
from jax import lax
from jax.experimental import pallas as pl
from jax.experimental.pallas import tpu as pltpu
from jax.sharding import PartitionSpec as P

D = 768
HD = 64
SEQ = 512
MESH = pl.DeviceIdType.MESH
F32 = jnp.float32
BF16 = jnp.bfloat16
FF_PIECES = 6
PIECES = 10
ORDERS = ("zyx", "yzx", "yzx", "xyz", "zyx", "yxz", "xyz", "xyz", "xyz", "xyz")
AFTER_HEAD = {
    0: ((1, 2), (2, 2), (0, 2), (3, 2)),
    1: ((4, 2),),
    3: ((1, 3), (5, 2)),
    4: ((0, 3), (6, 2)),
    5: ((1, 4), (2, 3)),
    6: ((3, 3),),
    7: ((5, 3),),
    8: ((3, 4), (4, 3), (1, 5)),
    9: ((5, 4), (6, 3), (7, 2)),
    10: ((0, 4),),
    11: ((1, 6), (2, 4)),
}
AFTER_LAST = (
    (3, 5), (7, 3), (6, 4), (5, 5), (8, 2), (1, 7), (4, 4), (3, 6),
    (8, 3), (2, 5), (7, 4), (3, 7), (9, 2), (5, 6), (0, 5), (6, 5),
    (8, 4), (4, 5), (2, 6), (9, 3), (7, 5), (5, 7), (9, 4), (8, 5),
    (7, 6), (4, 6), (-1, 0), (0, 6), (6, 6), (8, 6), (9, 5), (2, 7),
    (4, 7), (7, 7), (6, 7), (9, 6), (8, 7), (0, 7), (9, 7),
)


def flip(value, bit):
    return value + bit - 2 * bit * lax.rem(value // bit, 2)


def dot_nn(a, b):
    return lax.dot_general(a, b, (((1,), (0,)), ((), ())), preferred_element_type=F32)


def dot_nt(a, b):
    return lax.dot_general(a, b, (((1,), (1,)), ((), ())), preferred_element_type=F32)


def dot_tn(a, b):
    return lax.dot_general(a, b, (((0,), (0,)), ((), ())), preferred_element_type=F32)


def row_mean(value):
    return jnp.sum(value, -1, keepdims=True) * (1.0 / D)


def col_sum(value):
    return jnp.sum(value, 0, keepdims=True)


def norm_back(grad, normed, inv_std):
    return inv_std * (grad - row_mean(grad) - normed * row_mean(grad * normed))


def block(index, size):
    return pl.ds(pl.multiple_of(index * size, size), size)


def layer_kernel(dp_bits, tok_hbm, cot_hbm, len_ref, cnt_ref, qkv_own, out_own, up_own, down_own,
                 rows_ref, layer_out, grad_out, off_ref, oat_ref, vec_out,
                 wqkv, wo, wup, wdn, bias, tok, cot, qkv, ctx, lse, n1, r1, flow, hid, gd, gr2,
                 glow, acc, gctx, st, stage_rows, gff, r0, r1f, r2, r3, rx, rxa, vec_acc, vec_in,
                 ws, wr, gs, gr, vs, vr, os, orr, bs, br, ls, free_sem):
    t = lax.axis_index("tensor")
    d = lax.axis_index("dp")
    c = lax.rem(t, 2)
    x = t // 2
    b0 = lax.rem(d, 2)
    b1 = lax.rem(d // 2, 2)
    other = flip(t, 2)
    core = {"tensor": flip(t, 1)}
    across = {"tensor": other}
    dps = [{"dp": flip(d, 1 << k)} for k in range(dp_bits)]
    beside = dps[0]
    partners = (core, across, *dps)

    def send(src, dst, send_sem, recv_sem, device):
        return pltpu.make_async_remote_copy(
            src_ref=src, dst_ref=dst, send_sem=send_sem, recv_sem=recv_sem,
            device_id=device, device_id_type=MESH,
        )

    def slot_of(order):
        oc = lax.rem(order, 2)
        ox = order // 2
        return (x + ox - 2 * x * ox) * 2 + c + oc - 2 * c * oc

    loads = [
        pltpu.make_async_copy(tok_hbm.at[block(t, SEQ)], tok, ls.at[0]),
        pltpu.make_async_copy(qkv_own, wqkv.at[t], ls.at[1]),
        pltpu.make_async_copy(out_own, wo.at[t], ls.at[2]),
        pltpu.make_async_copy(up_own, wup.at[t], ls.at[3]),
        pltpu.make_async_copy(down_own, wdn.at[t], ls.at[4]),
        pltpu.make_async_copy(cot_hbm.at[block(t, SEQ)], cot, ls.at[5]),
    ]
    for load in loads:
        load.start()
    bias[t] = rows_ref[8:16]
    barrier = pltpu.get_barrier_semaphore()
    for device in partners:
        pl.semaphore_signal(barrier, inc=1, device_id=device, device_id_type=MESH)
    pl.semaphore_wait(barrier, len(partners))

    mine8 = rows_ref.at[pl.ds(8, 8)]
    bias_hop = send(mine8, bias.at[t], bs.at[0], br.at[0], across)
    bias_chip = send(mine8, bias.at[t], bs.at[1], br.at[1], core)
    bias_mate = send(bias.at[other], bias.at[other], bs.at[2], br.at[2], core)
    bias_hop.start()
    bias_chip.start()

    half_up = up_own.shape[0] // 2
    half_down = down_own.shape[0] // 2
    chunks = [
        (qkv_own, wqkv, 0, qkv_own.shape[0]), (out_own, wo, 0, out_own.shape[0]),
        (up_own, wup, 0, half_up), (up_own, wup, half_up, half_up),
        (down_own, wdn, 0, half_down), (down_own, wdn, half_down, half_down),
    ]

    def span(base, rows, which):
        return pl.ds(pl.multiple_of(base + which * (rows // 2), 16), rows // 2)

    hops, chips, relays, mates, lasts = [], [], [], [], []
    for i, (own, full, base, rows) in enumerate(chunks):
        hops.append(send(own.at[span(base, rows, b0)], full.at[t, span(base, rows, b0)],
                         ws.at[i, 1], wr.at[i, 1], across))
        chips.append(send(own.at[pl.ds(base, rows)], full.at[t, pl.ds(base, rows)],
                          ws.at[i, 0], wr.at[i, 0], core))
        here = full.at[other, span(base, rows, b0)]
        there = full.at[other, span(base, rows, 1 - b0)]
        relays.append(send(here, here, ws.at[i, 2], wr.at[i, 2], beside))
        mates.append(send(here, here, ws.at[i, 3], wr.at[i, 3], core))
        lasts.append(send(there, there, ws.at[i, 4], wr.at[i, 4], core))
        hops[i].start()
        chips[i].start()

    def from_across(i):
        hops[i].wait()
        relays[i].start()
        mates[i].start()

    def from_beside(i):
        relays[i].wait()
        lasts[i].start()

    def from_core(i):
        chips[i].wait()

    def from_far(i):
        mates[i].wait()
        lasts[i].wait()

    live = jnp.where(t < cnt_ref[0], 1.0, 0.0).astype(F32)
    length = len_ref[t]
    key_mask = jnp.where(
        lax.broadcasted_iota(jnp.int32, (1, SEQ), 1) < length, 0.0, -1e30
    ).astype(F32)
    vec_acc[0] = jnp.zeros_like(vec_acc[0])
    vec = vec_acc.at[0]

    def add_vec(row, value):
        vec[pl.ds(row, 1)] = vec[pl.ds(row, 1)] + value

    loads[0].wait()
    loads[1].wait()

    def attend(order, carry):
        s = slot_of(order)

        @pl.when(order == 1)
        def _():
            from_across(0)
            bias_hop.wait()
            bias_mate.start()
            from_core(0)
            bias_chip.wait()

        @pl.when(order == 2)
        def _():
            from_across(1)
            from_beside(0)
            bias_mate.wait()

        @pl.when(order == 3)
        def _():
            from_beside(1)
            from_far(0)

        for j in range(3):
            h = 3 * s + j
            w_rows = wqkv[s, 192 * j:192 * (j + 1)]
            qkv[h] = (dot_nt(tok[...], w_rows) + bias[s, 1 + j:2 + j, 0:192]).astype(BF16)
            keys = qkv[h, :, 64:128]
            values = qkv[h, :, 128:192]

            def rows(rb, carry):
                at = block(rb, 256)
                scores = dot_nt(qkv[h, at, 0:64], keys) * 0.125 + key_mask
                top = jnp.max(scores, -1, keepdims=True)
                expd = jnp.exp(scores - top)
                total = jnp.sum(expd, -1, keepdims=True)
                probs = (expd * (1.0 / total)).astype(BF16)
                ctx[s, at, 64 * j:64 * (j + 1)] = dot_nn(probs, values).astype(BF16)
                lane = lax.broadcasted_iota(jnp.int32, (256, 128), 1)
                lse[s, at] = jnp.where(lane == j, top + jnp.log(total), lse[s, at])
                return carry

            lax.fori_loop(0, SEQ // 256, rows, 0, unroll=True)
        return carry

    lse[...] = jnp.zeros_like(lse)
    lax.fori_loop(0, 4, attend, 0)

    from_across(2)
    from_core(1)
    from_far(1)
    loads[2].wait()
    gain1 = rows_ref[1:2]
    shift1 = rows_ref[2:3]

    def project(rb, carry):
        at = block(rb, 128)
        total = tok[at].astype(F32) + rows_ref[0:1]
        for s in range(4):
            total = total + dot_nn(ctx[s, at], wo[s])
        center = total - row_mean(total)
        inv = lax.rsqrt(row_mean(center * center) + 1e-5)
        normed = center * inv
        out = normed * gain1 + shift1
        n1[at] = normed
        r1[at] = inv
        flow[at] = out.astype(BF16)
        acc[at] = out + rows_ref[3:4]
        return carry

    lax.fori_loop(0, 4, project, 0)

    from_across(3)
    loads[3].wait()

    def raise_up(order, carry):
        s = slot_of(order)

        @pl.when(order == 1)
        def _():
            from_beside(2)
            from_core(2)
            from_core(3)

        @pl.when(order == 2)
        def _():
            from_across(4)
            from_beside(3)

        @pl.when(order == 3)
        def _():
            from_far(2)
            from_far(3)

        def rows(rb, carry):
            at = block(rb, 128)
            pre = dot_nn(flow[at], wup[s]) + bias[s, 0:1]
            cdf = 0.5 + 0.5 * lax.erf(pre * 0.7071067811865476)
            pdf = jnp.exp(pre * pre * -0.5) * 0.3989422804014327
            hid[s, at] = (pre * cdf).astype(BF16)
            gd[s, at] = (cdf + pre * pdf).astype(BF16)
            return carry

        lax.fori_loop(0, 4, rows, 0)
        return carry

    lax.fori_loop(0, 4, raise_up, 0)
    from_across(5)
    from_beside(4)
    loads[4].wait()

    def bring_down(order, carry):
        s = slot_of(order)

        @pl.when(order == 1)
        def _():
            from_core(4)
            from_core(5)

        @pl.when(order == 2)
        def _():
            from_beside(5)

        @pl.when(order == 3)
        def _():
            from_far(4)
            from_far(5)

        def rows(rb, carry):
            at = block(rb, 256)
            acc[at] = acc[at] + dot_nn(hid[s, at], wdn[s])
            return carry

        lax.fori_loop(0, 2, rows, 0)
        return carry

    lax.fori_loop(0, 4, bring_down, 0)

    loads[5].wait()
    gain2 = rows_ref[4:5]
    shift2 = rows_ref[5:6]
    lay = stage_rows.at[0]
    gtok = stage_rows.at[1]

    def second(rb, carry):
        at = block(rb, 128)
        total = acc[at]
        center = total - row_mean(total)
        inv = lax.rsqrt(row_mean(center * center) + 1e-5)
        normed = center * inv
        lay[at] = (live * (normed * gain2 + shift2)).astype(BF16)
        grad = live * cot[at].astype(F32)
        add_vec(1, col_sum(grad * normed))
        add_vec(2, col_sum(grad))
        back = norm_back(grad * gain2, normed, inv)
        low = back.astype(BF16)
        gr2[at] = back
        glow[at] = low
        add_vec(0, col_sum(low.astype(F32)))
        acc[at] = jnp.zeros_like(total)
        return carry

    lax.fori_loop(0, 4, second, 0)

    def spread(i, src, dst):
        return (
            pltpu.make_async_copy(src, dst.at[t], ls.at[6 + i]),
            send(src, dst.at[t], os.at[i, 0], orr.at[i, 0], across),
            send(src, dst.at[t], os.at[i, 1], orr.at[i, 1], core),
            send(dst.at[other], dst.at[other], os.at[i, 2], orr.at[i, 2], core),
        )

    lay_copies = spread(0, lay, layer_out)
    for copy in lay_copies[:3]:
        copy.start()

    n_exchange = dp_bits - 2
    last = 4 + n_exchange + 2

    def att_rows(shard, quarter, count):
        return pl.ds(pl.multiple_of((shard * 4 + quarter) * 48, 48), count)

    mine = {"x": x, "y": b0, "z": b1}
    peer = {"x": across, "y": dps[0], "z": dps[1]}
    got_ff = (r0, r1f, r2, r3)
    all_rows = slice(None)

    def halves(piece, s):
        if piece < FF_PIECES:
            place = {axis: mine[axis] for axis in ORDERS[piece][:max(s - 1, 0)]}
            at = [piece, c] + [place.get(axis, all_rows) for axis in "xyz"]
            away, keep = list(at), list(at)
            if s == 0:
                away[1] = 1 - c
            else:
                axis = ORDERS[piece][s - 1]
                away["xyz".index(axis) + 2] = 1 - mine[axis]
                keep["xyz".index(axis) + 2] = mine[axis]
            return gff.at[tuple(away)], gff.at[tuple(keep)], got_ff[s].at[piece]
        g = wdn.at[piece - FF_PIECES]
        r = wup.at[piece - FF_PIECES]
        me = 2 * c + x
        if s == 0:
            return g.at[att_rows(2 * (1 - c), 0, 384)], g.at[att_rows(2 * c, 0, 384)], r.at[pl.ds(0, 384)]
        if s == 1:
            return g.at[att_rows(2 * c + 1 - x, 0, 192)], g.at[att_rows(me, 0, 192)], r.at[pl.ds(384, 192)]
        if s == 2:
            return (g.at[att_rows(me, 2 * (1 - b0), 96)], g.at[att_rows(me, 2 * b0, 96)],
                    r.at[pl.ds(576, 96)])
        return (g.at[att_rows(me, 2 * b0 + 1 - b1, 48)], g.at[att_rows(me, 2 * b0 + b1, 48)],
                r.at[pl.ds(672, 48)])

    def kept(piece):
        if piece < FF_PIECES:
            return gff.at[piece, c, x, b0, b1], rx.at[piece], off_ref.at[piece]
        own = wdn.at[piece - FF_PIECES, att_rows(2 * c + x, 2 * b0 + b1, 48)]
        return own, rxa.at[piece - FF_PIECES], oat_ref.at[piece - FF_PIECES]

    def stage_copy(s, piece):
        sems = (gs.at[s, piece], gr.at[s, piece])
        order = ORDERS[piece]
        if s < 4:
            away, _, got = halves(piece, s)
            return send(away, got, *sems, core if s == 0 else peer[order[s - 1]])
        own, got, out = kept(piece)
        if s < 4 + n_exchange:
            return send(own, got.at[s - 4], *sems, dps[s - 2])
        back = [axis for axis in order if axis != "x"]
        if s == 4 + n_exchange:
            part = out.at[b0, b1]
            return send(part, part, *sems, peer[back[1]])
        part = out.at[b0] if back[0] == "y" else out.at[:, b1]
        return send(part, part, *sems, peer[back[0]])

    def combine(s, piece):
        if s < 4:
            _, keep, got = halves(piece, s)
            keep[...] = keep[...] + got[...]
        elif s < 4 + n_exchange:
            own, got, out = kept(piece)
            total = own[...] + got[s - 4]
            if s == 3 + n_exchange:
                out[b0, b1] = total
            else:
                own[...] = total

    def run_stage(s, piece):
        if s > 0:
            stage_copy(s - 1, piece).wait()
            combine(s - 1, piece)
        if s < last:
            stage_copy(s, piece).start()

    def late_stage(piece, s):
        if s < 5:
            run_stage(s, piece)
        elif s == 5:
            for k in range(5, 5 + n_exchange):
                run_stage(k, piece)
        else:
            run_stage(s + n_exchange - 1, piece)

    def down_grad(i, carry):
        def shard(s, carry):
            value = dot_tn(hid[s, :, block(i, 256)], glow[...]).astype(BF16)
            for q in range(4):
                gff[i, lax.rem(s, 2), s // 2, q // 2, q % 2] = value[64 * q:64 * (q + 1)]
            return carry

        lax.fori_loop(0, 4, shard, 0)
        for k in range(3):
            @pl.when(i == k)
            def _():
                run_stage(0, k)
                if k > 0:
                    run_stage(1, k - 1)

        return carry

    lax.fori_loop(0, 3, down_grad, 0)

    def ffn_back(s, carry):
        @pl.when(s == 1)
        def _():
            run_stage(1, 2)
            lay_copies[1].wait()
            lay_copies[3].start()

        def rows(rb, carry):
            at = block(rb, 256)
            low = (dot_nt(glow[at], wdn[s]) * gd[s, at].astype(F32)).astype(BF16)
            gd[s, at] = low
            add_vec(8 + s, col_sum(low.astype(F32)))
            acc[at] = acc[at] + dot_nt(low, wup[s])
            return carry

        lax.fori_loop(0, 2, rows, 0)
        return carry

    lax.fori_loop(0, 4, ffn_back, 0)
    for device in partners:
        pl.semaphore_signal(free_sem, inc=1, device_id=device, device_id_type=MESH)

    def up_grad(i, carry):
        def shard(s, carry):
            value = dot_tn(flow[:, block(i, 256)], gd[s]).astype(BF16)
            for q in range(4):
                gff[3 + i, lax.rem(s, 2), s // 2, q // 2, q % 2] = value[64 * q:64 * (q + 1)]
            return carry

        lax.fori_loop(0, 4, shard, 0)
        for k in range(3):
            @pl.when(i == k)
            def _():
                run_stage(0, 3 + k)
                if k > 0:
                    run_stage(1, 2 + k)

        return carry

    lax.fori_loop(0, 3, up_grad, 0)

    def first_back(rb, carry):
        at = block(rb, 128)
        grad = gr2[at] + acc[at]
        normed = n1[at]
        add_vec(4, col_sum(grad * normed))
        add_vec(5, col_sum(grad))
        back = norm_back(grad * gain1, normed, r1[at])
        low = back.astype(BF16)
        acc[at] = back
        glow[at] = low
        add_vec(3, col_sum(low.astype(F32)))
        return carry

    lax.fori_loop(0, 4, first_back, 0)
    run_stage(1, 5)

    pl.semaphore_wait(free_sem, len(partners))

    def out_back(s, carry):
        home = att_rows(2 * lax.rem(s, 2) + s // 2, 0, 192)
        wdn[0, home] = dot_tn(ctx[s], glow[...]).astype(BF16)
        back = dot_nt(glow[...], wo[s]).astype(BF16)
        for j in range(3):
            gctx[3 * s + j] = back[:, 64 * j:64 * (j + 1)]
        return carry

    lax.fori_loop(0, 4, out_back, 0)
    run_stage(0, 6)

    def head_back(n, carry):
        s = slot_of(lax.rem(n, 4))
        j = n // 4
        h = 3 * s + j
        keys = qkv[h, :, 64:128]
        values = qkv[h, :, 128:192]
        keys_t = keys.T
        st[...] = jnp.zeros_like(st)

        def rows(rb, carry):
            at = block(rb, 256)
            query = qkv[h, at, 0:64]
            gout = gctx[h, at]
            lane = lax.broadcasted_iota(jnp.int32, (256, 128), 1)
            norm = jnp.sum(jnp.where(lane == j, lse[s, at], 0.0), -1, keepdims=True)
            probs = jnp.exp(dot_nt(query, keys) * 0.125 + key_mask - norm)
            gprobs = dot_nt(gout, values)
            scored = probs * (gprobs - jnp.sum(gprobs * probs, -1, keepdims=True))
            scored = scored.astype(BF16)
            st[0:64, at] = dot_nt(keys_t, scored)
            st[64:128] = st[64:128] + dot_tn(query, scored)
            st[128:192] = st[128:192] + dot_tn(gout, probs.astype(BF16))
            return carry

        lax.fori_loop(0, SEQ // 256, rows, 0, unroll=True)
        row = lax.broadcasted_iota(jnp.int32, (192, 1), 0)
        packed = (st[...] * jnp.where(row < 128, 0.125, 1.0)).astype(BF16)
        home = att_rows(2 * lax.rem(s, 2) + s // 2, 0, 192)
        wdn[1 + j, home] = dot_nn(packed, tok[...]).astype(BF16)
        sums = dot_nt(jnp.ones((8, SEQ), BF16), packed)
        vec[pl.ds(12 + h, 1), 0:192] = sums[0:1]
        w_rows = wqkv[s, block(j, 192)]

        acc[...] = acc[...] + dot_tn(packed, w_rows)

        for k in range(12):
            @pl.when(n == k)
            def _():
                if k % 4 == 0:
                    run_stage(1, 6 + k // 4)
                if k % 4 == 3:
                    run_stage(0, 7 + k // 4)
                for piece, s in AFTER_HEAD.get(k, ()):
                    late_stage(piece, s)

        return carry

    lax.fori_loop(0, 12, head_back, 0)
    gtok[...] = acc[...].astype(BF16)
    run_stage(1, 9)
    tok_copies = spread(1, gtok, grad_out)
    for copy in tok_copies[:3]:
        copy.start()

    def vec_copy(k):
        return send(vec_acc.at[k], vec_in.at[k], vs.at[k], vr.at[k], partners[k])

    def vec_step(k):
        if k > 0:
            vec_copy(k - 1).wait()
            total = vec_acc[k - 1] + vec_in[k - 1]
            if k == len(partners):
                vec_out[...] = total
                return
            vec_acc[k] = total
        vec_copy(k).start()

    vec_step(0)
    steps = 1
    for i, (piece, s) in enumerate(AFTER_LAST):
        if piece < 0:
            tok_copies[1].wait()
            tok_copies[3].start()
        else:
            late_stage(piece, s)
        if i % 4 == 3 and steps <= len(partners):
            vec_step(steps)
            steps += 1
    while steps <= len(partners):
        vec_step(steps)
        steps += 1
    for copies in (lay_copies, tok_copies):
        copies[0].wait()
        copies[2].wait()
        copies[3].wait()


def run_layer(dp, tokens, cotangent, key_lengths, slot_counts, shards, rows):
    dp_bits = dp.bit_length() - 1
    n_exchange = dp_bits - 2
    stages = 4 + n_exchange + 2
    links = dp_bits + 2
    vmem = pl.BlockSpec(memory_space=pltpu.VMEM)
    smem = pl.BlockSpec(memory_space=pltpu.SMEM)
    hbm = pl.BlockSpec(memory_space=pltpu.HBM)
    dma = pltpu.SemaphoreType.DMA
    return pl.pallas_call(
        functools.partial(layer_kernel, dp_bits),
        out_shape=[
            jax.ShapeDtypeStruct((4, SEQ, D), BF16),
            jax.ShapeDtypeStruct((4, SEQ, D), BF16),
            jax.ShapeDtypeStruct((6, 2, 2, 64, D), BF16),
            jax.ShapeDtypeStruct((4, 2, 2, 48, D), BF16),
            jax.ShapeDtypeStruct((24, D), F32),
        ],
        in_specs=[hbm, hbm, smem, smem] + [hbm] * 4 + [vmem],
        out_specs=[hbm] * 2 + [vmem] * 3,
        scratch_shapes=[
            *[pltpu.VMEM((4, *s.shape), BF16) for s in shards],
            pltpu.VMEM((4, 8, D), F32),
            pltpu.VMEM((SEQ, D), BF16),
            pltpu.VMEM((SEQ, D), BF16),
            pltpu.VMEM((12, SEQ, 192), BF16),
            pltpu.VMEM((4, SEQ, 192), BF16),
            pltpu.VMEM((4, SEQ, 128), F32),
            pltpu.VMEM((SEQ, D), F32),
            pltpu.VMEM((SEQ, 1), F32),
            pltpu.VMEM((SEQ, D), BF16),
            pltpu.VMEM((4, SEQ, D), BF16),
            pltpu.VMEM((4, SEQ, D), BF16),
            pltpu.VMEM((SEQ, D), F32),
            pltpu.VMEM((SEQ, D), BF16),
            pltpu.VMEM((SEQ, D), F32),
            pltpu.VMEM((12, SEQ, 64), BF16),
            pltpu.VMEM((192, SEQ), F32),
            pltpu.VMEM((2, SEQ, D), BF16),
            pltpu.VMEM((6, 2, 2, 2, 2, 64, D), BF16),
            pltpu.VMEM((6, 2, 2, 2, 64, D), BF16),
            pltpu.VMEM((6, 2, 2, 64, D), BF16),
            pltpu.VMEM((6, 2, 64, D), BF16),
            pltpu.VMEM((6, 64, D), BF16),
            pltpu.VMEM((6, n_exchange, 64, D), BF16),
            pltpu.VMEM((4, n_exchange, 48, D), BF16),
            pltpu.VMEM((links, 24, D), F32),
            pltpu.VMEM((links, 24, D), F32),
            dma((6, 5)), dma((6, 5)),
            dma((stages, PIECES)), dma((stages, PIECES)),
            dma((links,)), dma((links,)),
            dma((2, 3)), dma((2, 3)),
            dma((3,)), dma((3,)),
            dma((8,)),
            pltpu.SemaphoreType.REGULAR,
        ],
        compiler_params=pltpu.CompilerParams(
            collective_id=0, has_side_effects=True, vmem_limit_bytes=67043328
        ),
    )(tokens, cotangent, key_lengths, slot_counts, *shards, rows)


def per_device(dp, tokens, cotangent, key_lengths, slot_counts, *params):
    (w_query, b_query, w_key, w_value, b_value, w_out, b_out, attn_gain, attn_shift,
     w_up, b_up, w_down, b_down, ffn_gain, ffn_shift) = params
    slot = lax.axis_index("tensor")
    heads = w_query.shape[1] // HD
    qkv = jnp.stack([w.reshape(D, heads, HD) for w in (w_query, w_key, w_value)], 1)
    qkv = qkv.transpose(2, 1, 3, 0).reshape(-1, D)
    q_bias = b_query.reshape(heads, HD)
    v_bias = b_value.reshape(heads, HD)
    qkv_bias = jnp.concatenate(
        (q_bias, jnp.zeros_like(q_bias), v_bias, jnp.zeros((heads, D - 3 * HD), BF16)), 1
    )
    rows = jnp.concatenate(
        [v[None] for v in (b_out, attn_gain, attn_shift, b_down, ffn_gain, ffn_shift)]
        + [jnp.zeros((2, D), BF16), b_up[None], qkv_bias, jnp.zeros((4, D), BF16)], 0
    ).astype(F32)
    layer, grad, off, oat, vec = run_layer(
        dp, tokens, cotangent, key_lengths, slot_counts, (qkv, w_out, w_up, w_down), rows
    )
    off = off.reshape(2, -1, D).astype(F32)
    oat = oat.reshape(4, -1, D)
    g_out = oat[0].astype(F32)
    g_qkv = oat[1:].reshape(heads, 3, HD, D)
    g_q, g_k, g_v = (g_qkv[:, i].reshape(-1, D).T.astype(F32) for i in range(3))
    b_qkv = lax.dynamic_slice_in_dim(vec[12:, :3 * HD], slot * heads, heads)
    gb_up = lax.dynamic_slice_in_dim(vec[8:12], slot, 1)[0]
    return (layer.reshape(-1, D), grad.reshape(-1, D),
            g_q, b_qkv[:, :HD].reshape(-1), g_k, g_v, b_qkv[:, 2 * HD:].reshape(-1), g_out,
            vec[3], vec[4], vec[5], off[1], gb_up, off[0], vec[0], vec[1], vec[2])


def solution(mesh):
    placed = (
        P("dp", None),
        P("dp", None),
        P("dp"),
        P("dp"),
        P(None, "tensor"),
        P("tensor"),
        P(None, "tensor"),
        P(None, "tensor"),
        P("tensor"),
        P("tensor", None),
        P(),
        P(),
        P(),
        P(None, "tensor"),
        P("tensor"),
        P("tensor", None),
        P(),
        P(),
        P(),
    )
    return jax.shard_map(
        functools.partial(per_device, mesh.shape["dp"]),
        mesh=mesh,
        in_specs=placed,
        out_specs=(
            P("dp", None),
            P("dp", None),
            P(None, "tensor"),
            P("tensor"),
            P(None, "tensor"),
            P(None, "tensor"),
            P("tensor"),
            P("tensor", None),
            P(),
            P(),
            P(),
            P(None, "tensor"),
            P("tensor"),
            P("tensor", None),
            P(),
            P(),
            P(),
        ),
        check_vma=False,
    )
```

```python
import functools

import jax
import jax.numpy as jnp
from jax import lax
from jax.experimental import pallas as pl
from jax.experimental.pallas import tpu as pltpu
from jax.sharding import PartitionSpec as P

D = 768
HD = 64
SEQ = 512
MESH = pl.DeviceIdType.MESH
F32 = jnp.float32
BF16 = jnp.bfloat16
FF_PIECES = 6
PIECES = 10
ORDERS = ("yxz", "yzx", "xyz", "zxy", "yzx", "xyz", "xyz", "xyz", "xyz", "xyz")
AFTER_HEAD = {
    0: ((0, 2), (2, 2), (1, 2), (3, 2)),
    1: ((4, 2),),
    3: ((5, 2),),
    4: ((2, 3), (1, 3)),
    6: ((4, 3), (5, 3), (6, 2)),
    7: ((2, 4),),
    8: ((0, 3), (5, 4)),
    9: ((6, 3), (3, 3)),
    11: ((0, 4), (2, 5)),
}
AFTER_LAST = (
    (5, 5), (6, 4), (7, 2), (1, 4), (2, 6), (0, 5), (4, 4), (5, 6),
    (7, 3), (3, 4), (2, 7), (6, 5), (8, 2), (0, 6), (5, 7), (-3, 2),
    (1, 5), (9, 2), (8, 3), (7, 4), (4, 5), (0, 7), (-3, 3), (6, 6),
    (1, 6), (8, 4), (9, 3), (3, 5), (-3, 4), (4, 6), (6, 7), (7, 5),
    (-1, 0), (1, 7), (9, 4), (8, 5), (-3, 5), (7, 6), (4, 7), (8, 6),
    (9, 5), (3, 6), (7, 7), (9, 6), (8, 7), (-2, 0), (9, 7), (3, 7),
)
VIA = (1, 0, 1, 0, 1, 1, 0, 1)
FETCH_HEAD = {(1, 2): ((0, 0),), (2, 0): ((0, 1), (0, 2)), (2, 2): ((0, 3),), (3, 1): ((1, 1),), (3, 2): ((0, 4),)}
FETCH_NORM = ((1, 2), (0, 5))
FETCH_UP = {1: ((1, 3),), 2: ((0, 6), (1, 4)), 3: ((0, 7),)}
FETCH_DOWN = {0: ((1, 5),)}


def flip(value, bit):
    return value + bit - 2 * bit * lax.rem(value // bit, 2)


def dot_nn(a, b):
    return lax.dot_general(a, b, (((1,), (0,)), ((), ())), preferred_element_type=F32)


def dot_nt(a, b):
    return lax.dot_general(a, b, (((1,), (1,)), ((), ())), preferred_element_type=F32)


def dot_tn(a, b):
    return lax.dot_general(a, b, (((0,), (0,)), ((), ())), preferred_element_type=F32)


def row_mean(value):
    return jnp.sum(value, -1, keepdims=True) * (1.0 / D)


def col_sum(value):
    return jnp.sum(value, 0, keepdims=True)


def norm_back(grad, normed, inv_std):
    return inv_std * (grad - row_mean(grad) - normed * row_mean(grad * normed))


def block(index, size):
    return pl.ds(pl.multiple_of(index * size, size), size)


def layer_kernel(dp_bits, tok_hbm, cot_hbm, len_ref, cnt_ref, qkv_own, out_own, up_own, down_own,
                 rows_ref, layer_out, grad_out, off_ref, oat_ref, vec_out,
                 wqkv, wo, wup, wdn, bias, tok, cot, qkv, ctx, lse, n1, r1, flow, hid, gd, gr2,
                 glow, acc, gctx, st, stage_rows, gff, r0, r1f, r2, r3, rx, rxa, vec_acc, vec_in,
                 ws, wr, gs, gr, vs, vr, os, orr, bs, br, ls, free_sem):
    t = lax.axis_index("tensor")
    d = lax.axis_index("dp")
    c = lax.rem(t, 2)
    x = t // 2
    b0 = lax.rem(d, 2)
    b1 = lax.rem(d // 2, 2)
    other = flip(t, 2)
    core = {"tensor": flip(t, 1)}
    across = {"tensor": other}
    dps = [{"dp": flip(d, 1 << k)} for k in range(dp_bits)]
    partners = (core, across, *dps)

    def send(src, dst, send_sem, recv_sem, device):
        return pltpu.make_async_remote_copy(
            src_ref=src, dst_ref=dst, send_sem=send_sem, recv_sem=recv_sem,
            device_id=device, device_id_type=MESH,
        )

    def slot_of(order):
        oc = lax.rem(order, 2)
        ox = order // 2
        return (x + ox - 2 * x * ox) * 2 + c + oc - 2 * c * oc

    loads = [
        pltpu.make_async_copy(tok_hbm.at[block(t, SEQ)], tok, ls.at[0]),
        pltpu.make_async_copy(qkv_own, wqkv.at[t], ls.at[1]),
        pltpu.make_async_copy(out_own, wo.at[t], ls.at[2]),
        pltpu.make_async_copy(up_own, wup.at[t], ls.at[3]),
        pltpu.make_async_copy(down_own, wdn.at[t], ls.at[4]),
        pltpu.make_async_copy(cot_hbm.at[block(t, SEQ)], cot, ls.at[5]),
    ]
    for load in loads:
        load.start()
    bias[t] = rows_ref[8:16]
    barrier = pltpu.get_barrier_semaphore()
    for device in partners:
        pl.semaphore_signal(barrier, inc=1, device_id=device, device_id_type=MESH)
    pl.semaphore_wait(barrier, len(partners))

    mine8 = rows_ref.at[pl.ds(8, 8)]
    bias_hop = send(mine8, bias.at[t], bs.at[0], br.at[0], across)
    bias_chip = send(mine8, bias.at[t], bs.at[1], br.at[1], core)
    bias_mate = send(bias.at[other], bias.at[other], bs.at[2], br.at[2], core)
    bias_hop.start()
    bias_chip.start()

    half_up = up_own.shape[0] // 2
    part_down = down_own.shape[0] // 4
    chunks = [
        (qkv_own, wqkv, 0, qkv_own.shape[0]), (out_own, wo, 0, out_own.shape[0]),
        (up_own, wup, 0, half_up), (up_own, wup, half_up, half_up),
        *[(down_own, wdn, k * part_down, part_down) for k in range(4)],
    ]

    def span(base, rows, which):
        return pl.ds(pl.multiple_of(base + which * (rows // 2), 16), rows // 2)

    hops, chips, relays, mates, lasts = [], [], [], [], []
    for i, (own, full, base, rows) in enumerate(chunks):
        bit = (b0, b1)[VIA[i]]
        hops.append(send(own.at[span(base, rows, bit)], full.at[t, span(base, rows, bit)],
                         ws.at[i, 1], wr.at[i, 1], across))
        chips.append(send(own.at[pl.ds(base, rows)], full.at[t, pl.ds(base, rows)],
                          ws.at[i, 0], wr.at[i, 0], core))
        here = full.at[other, span(base, rows, bit)]
        there = full.at[other, span(base, rows, 1 - bit)]
        relays.append(send(here, here, ws.at[i, 2], wr.at[i, 2], dps[VIA[i]]))
        mates.append(send(here, here, ws.at[i, 3], wr.at[i, 3], core))
        lasts.append(send(there, there, ws.at[i, 4], wr.at[i, 4], core))
        hops[i].start()
        chips[i].start()

    def from_across(i):
        hops[i].wait()
        relays[i].start()
        mates[i].start()

    def from_beside(i):
        relays[i].wait()
        lasts[i].start()

    def fetch(steps):
        for over_dp, i in steps:
            (from_beside if over_dp else from_across)(i)

    def from_core(i):
        chips[i].wait()

    def from_far(i):
        mates[i].wait()
        lasts[i].wait()

    live = jnp.where(t < cnt_ref[0], 1.0, 0.0).astype(F32)
    length = len_ref[t]
    key_mask = jnp.where(
        lax.broadcasted_iota(jnp.int32, (1, SEQ), 1) < length, 0.0, -1e30
    ).astype(F32)
    vec_acc[0] = jnp.zeros_like(vec_acc[0])
    vec = vec_acc.at[0]

    def add_vec(row, value):
        vec[pl.ds(row, 1)] = vec[pl.ds(row, 1)] + value

    loads[0].wait()
    loads[1].wait()

    def attend(order, carry):
        s = slot_of(order)

        @pl.when(order == 1)
        def _():
            bias_hop.wait()
            bias_mate.start()
            from_core(0)
            bias_chip.wait()

        @pl.when(order == 2)
        def _():
            from_beside(0)
            bias_mate.wait()

        @pl.when(order == 3)
        def _():
            from_far(0)

        for j in range(3):
            h = 3 * s + j
            w_rows = wqkv[s, 192 * j:192 * (j + 1)]
            qkv[h] = (dot_nt(tok[...], w_rows) + bias[s, 1 + j:2 + j, 0:192]).astype(BF16)
            keys = qkv[h, :, 64:128]
            values = qkv[h, :, 128:192]

            def rows(rb, carry):
                at = block(rb, 512)
                scores = dot_nt(qkv[h, at, 0:64], keys) * 0.125 + key_mask
                top = jnp.max(scores, -1, keepdims=True)
                expd = jnp.exp(scores - top)
                total = jnp.sum(expd, -1, keepdims=True)
                probs = (expd * (1.0 / total)).astype(BF16)
                ctx[s, at, 64 * j:64 * (j + 1)] = dot_nn(probs, values).astype(BF16)
                lane = lax.broadcasted_iota(jnp.int32, (512, 128), 1)
                lse[s, at] = jnp.where(lane == j, top + jnp.log(total), lse[s, at])
                return carry

            lax.fori_loop(0, SEQ // 512, rows, 0, unroll=True)
            for o in range(4):
                if (o, j) in FETCH_HEAD:
                    @pl.when(order == o)
                    def _():
                        fetch(FETCH_HEAD[(o, j)])
        return carry

    lse[...] = jnp.zeros_like(lse)
    lax.fori_loop(0, 4, attend, 0)

    from_core(1)
    from_far(1)
    loads[2].wait()
    gain1 = rows_ref[1:2]
    shift1 = rows_ref[2:3]

    def project(rb, carry):
        at = block(rb, 128)
        total = tok[at].astype(F32) + rows_ref[0:1]
        for s in range(4):
            total = total + dot_nn(ctx[s, at], wo[s])
        center = total - row_mean(total)
        inv = lax.rsqrt(row_mean(center * center) + 1e-5)
        normed = center * inv
        out = normed * gain1 + shift1
        n1[at] = normed
        r1[at] = inv
        flow[at] = out.astype(BF16)
        acc[at] = out + rows_ref[3:4]
        return carry

    lax.fori_loop(0, 4, project, 0)

    fetch(FETCH_NORM)
    loads[3].wait()

    def raise_up(order, carry):
        s = slot_of(order)

        @pl.when(order == 1)
        def _():
            from_core(2)
            from_core(3)

        @pl.when(order == 3)
        def _():
            from_far(2)
            from_far(3)

        def rows(rb, carry):
            at = block(rb, 128)
            pre = dot_nn(flow[at], wup[s]) + bias[s, 0:1]
            cdf = 0.5 + 0.5 * lax.erf(pre * 0.7071067811865476)
            pdf = jnp.exp(pre * pre * -0.5) * 0.3989422804014327
            hid[s, at] = (pre * cdf).astype(BF16)
            gd[s, at] = (cdf + pre * pdf).astype(BF16)
            return carry

        lax.fori_loop(0, 4, rows, 0)
        for o, steps in FETCH_UP.items():
            @pl.when(order == o)
            def _():
                fetch(steps)
        return carry

    lax.fori_loop(0, 4, raise_up, 0)
    loads[4].wait()

    def bring_down(order, carry):
        s = slot_of(order)

        @pl.when(order == 1)
        def _():
            for i in range(4, 8):
                from_core(i)

        @pl.when(order == 2)
        def _():
            from_beside(6)
            from_beside(7)

        @pl.when(order == 3)
        def _():
            for i in range(4, 8):
                from_far(i)

        def rows(rb, carry):
            at = block(rb, 256)
            acc[at] = acc[at] + dot_nn(hid[s, at], wdn[s])
            return carry

        lax.fori_loop(0, 2, rows, 0)
        for o, steps in FETCH_DOWN.items():
            @pl.when(order == o)
            def _():
                fetch(steps)
        return carry

    lax.fori_loop(0, 4, bring_down, 0)

    loads[5].wait()
    gain2 = rows_ref[4:5]
    shift2 = rows_ref[5:6]
    lay = stage_rows.at[0]
    gtok = stage_rows.at[1]

    def second(rb, carry):
        at = block(rb, 128)
        total = acc[at]
        center = total - row_mean(total)
        inv = lax.rsqrt(row_mean(center * center) + 1e-5)
        normed = center * inv
        lay[at] = (live * (normed * gain2 + shift2)).astype(BF16)
        grad = live * cot[at].astype(F32)
        add_vec(1, col_sum(grad * normed))
        add_vec(2, col_sum(grad))
        back = norm_back(grad * gain2, normed, inv)
        low = back.astype(BF16)
        gr2[at] = back
        glow[at] = low
        add_vec(0, col_sum(low.astype(F32)))
        acc[at] = jnp.zeros_like(total)
        return carry

    lax.fori_loop(0, 4, second, 0)

    def spread(i, src, dst):
        return (
            pltpu.make_async_copy(src, dst.at[t], ls.at[6 + i]),
            send(src, dst.at[t], os.at[i, 0], orr.at[i, 0], across),
            send(src, dst.at[t], os.at[i, 1], orr.at[i, 1], core),
            send(dst.at[other], dst.at[other], os.at[i, 2], orr.at[i, 2], core),
        )

    lay_copies = spread(0, lay, layer_out)
    lay_copies[0].start()
    lay_copies[2].start()

    n_exchange = dp_bits - 2
    last = 4 + n_exchange + 2

    def att_rows(shard, quarter, count):
        return pl.ds(pl.multiple_of((shard * 4 + quarter) * 48, 48), count)

    mine = {"x": x, "y": b0, "z": b1}
    peer = {"x": across, "y": dps[0], "z": dps[1]}
    got_ff = (r0, r1f, r2, r3)
    all_rows = slice(None)

    def halves(piece, s):
        if piece < FF_PIECES:
            place = {axis: mine[axis] for axis in ORDERS[piece][:max(s - 1, 0)]}
            at = [piece, c] + [place.get(axis, all_rows) for axis in "xyz"]
            away, keep = list(at), list(at)
            if s == 0:
                away[1] = 1 - c
            else:
                axis = ORDERS[piece][s - 1]
                away["xyz".index(axis) + 2] = 1 - mine[axis]
                keep["xyz".index(axis) + 2] = mine[axis]
            return gff.at[tuple(away)], gff.at[tuple(keep)], got_ff[s].at[piece]
        g = wdn.at[piece - FF_PIECES]
        r = wup.at[piece - FF_PIECES]
        me = 2 * c + x
        if s == 0:
            return g.at[att_rows(2 * (1 - c), 0, 384)], g.at[att_rows(2 * c, 0, 384)], r.at[pl.ds(0, 384)]
        if s == 1:
            return g.at[att_rows(2 * c + 1 - x, 0, 192)], g.at[att_rows(me, 0, 192)], r.at[pl.ds(384, 192)]
        if s == 2:
            return (g.at[att_rows(me, 2 * (1 - b0), 96)], g.at[att_rows(me, 2 * b0, 96)],
                    r.at[pl.ds(576, 96)])
        return (g.at[att_rows(me, 2 * b0 + 1 - b1, 48)], g.at[att_rows(me, 2 * b0 + b1, 48)],
                r.at[pl.ds(672, 48)])

    def kept(piece):
        if piece < FF_PIECES:
            return gff.at[piece, c, x, b0, b1], rx.at[piece], off_ref.at[piece]
        own = wdn.at[piece - FF_PIECES, att_rows(2 * c + x, 2 * b0 + b1, 48)]
        return own, rxa.at[piece - FF_PIECES], oat_ref.at[piece - FF_PIECES]

    def stage_copy(s, piece):
        sems = (gs.at[s, piece], gr.at[s, piece])
        order = ORDERS[piece]
        if s < 4:
            away, _, got = halves(piece, s)
            return send(away, got, *sems, core if s == 0 else peer[order[s - 1]])
        own, got, out = kept(piece)
        if s < 4 + n_exchange:
            return send(own, got.at[s - 4], *sems, dps[s - 2])
        back = [axis for axis in order if axis != "x"]
        if s == 4 + n_exchange:
            part = out.at[b0, b1]
            return send(part, part, *sems, peer[back[1]])
        part = out.at[b0] if back[0] == "y" else out.at[:, b1]
        return send(part, part, *sems, peer[back[0]])

    def combine(s, piece):
        if s < 4:
            _, keep, got = halves(piece, s)
            keep[...] = keep[...] + got[...]
        elif s < 4 + n_exchange:
            own, got, out = kept(piece)
            total = own[...] + got[s - 4]
            if s == 3 + n_exchange:
                out[b0, b1] = total
            else:
                own[...] = total

    def run_stage(s, piece):
        if s > 0:
            stage_copy(s - 1, piece).wait()
            combine(s - 1, piece)
        if s < last:
            stage_copy(s, piece).start()

    def late_stage(piece, s):
        if s < 5:
            run_stage(s, piece)
        elif s == 5:
            for k in range(5, 5 + n_exchange):
                run_stage(k, piece)
        else:
            run_stage(s + n_exchange - 1, piece)

    def down_grad(i, carry):
        def shard(s, carry):
            value = dot_tn(hid[s, :, block(i, 256)], glow[...]).astype(BF16)
            for q in range(4):
                gff[i, lax.rem(s, 2), s // 2, q // 2, q % 2] = value[64 * q:64 * (q + 1)]
            return carry

        lax.fori_loop(0, 4, shard, 0)
        for k in range(3):
            @pl.when(i == k)
            def _():
                run_stage(0, k)
                if k > 0:
                    run_stage(1, k - 1)

        return carry

    lax.fori_loop(0, 3, down_grad, 0)

    def ffn_back(s, carry):
        @pl.when(s == 1)
        def _():
            run_stage(1, 2)

        def rows(rb, carry):
            at = block(rb, 256)
            low = (dot_nt(glow[at], wdn[s]) * gd[s, at].astype(F32)).astype(BF16)
            gd[s, at] = low
            add_vec(8 + s, col_sum(low.astype(F32)))
            acc[at] = acc[at] + dot_nt(low, wup[s])
            return carry

        lax.fori_loop(0, 2, rows, 0)
        return carry

    lax.fori_loop(0, 4, ffn_back, 0)
    for device in partners:
        pl.semaphore_signal(free_sem, inc=1, device_id=device, device_id_type=MESH)

    def up_grad(i, carry):
        def shard(s, carry):
            value = dot_tn(flow[:, block(i, 256)], gd[s]).astype(BF16)
            for q in range(4):
                gff[3 + i, lax.rem(s, 2), s // 2, q // 2, q % 2] = value[64 * q:64 * (q + 1)]
            return carry

        lax.fori_loop(0, 4, shard, 0)
        for k in range(3):
            @pl.when(i == k)
            def _():
                run_stage(0, 3 + k)
                if k > 0:
                    run_stage(1, 2 + k)

        return carry

    lax.fori_loop(0, 3, up_grad, 0)

    def first_back(rb, carry):
        at = block(rb, 128)
        grad = gr2[at] + acc[at]
        normed = n1[at]
        add_vec(4, col_sum(grad * normed))
        add_vec(5, col_sum(grad))
        back = norm_back(grad * gain1, normed, r1[at])
        low = back.astype(BF16)
        acc[at] = back
        glow[at] = low
        add_vec(3, col_sum(low.astype(F32)))
        return carry

    lax.fori_loop(0, 4, first_back, 0)
    run_stage(1, 5)

    pl.semaphore_wait(free_sem, len(partners))

    def out_back(s, carry):
        home = att_rows(2 * lax.rem(s, 2) + s // 2, 0, 192)
        wdn[0, home] = dot_tn(ctx[s], glow[...]).astype(BF16)
        back = dot_nt(glow[...], wo[s]).astype(BF16)
        for j in range(3):
            gctx[3 * s + j] = back[:, 64 * j:64 * (j + 1)]
        return carry

    lax.fori_loop(0, 4, out_back, 0)
    run_stage(0, 6)

    def head_back(n, carry):
        s = slot_of(lax.rem(n, 4))
        j = n // 4
        h = 3 * s + j
        keys = qkv[h, :, 64:128]
        values = qkv[h, :, 128:192]
        keys_t = keys.T
        st[...] = jnp.zeros_like(st)

        def rows(rb, carry):
            at = block(rb, 512)
            query = qkv[h, at, 0:64]
            gout = gctx[h, at]
            lane = lax.broadcasted_iota(jnp.int32, (512, 128), 1)
            norm = jnp.sum(jnp.where(lane == j, lse[s, at], 0.0), -1, keepdims=True)
            probs = jnp.exp(dot_nt(query, keys) * 0.125 + key_mask - norm)
            gprobs = dot_nt(gout, values)
            scored = probs * (gprobs - jnp.sum(gprobs * probs, -1, keepdims=True))
            scored = scored.astype(BF16)
            st[0:64, at] = dot_nt(keys_t, scored)
            st[64:128] = st[64:128] + dot_tn(query, scored)
            st[128:192] = st[128:192] + dot_tn(gout, probs.astype(BF16))
            return carry

        lax.fori_loop(0, SEQ // 512, rows, 0, unroll=True)
        row = lax.broadcasted_iota(jnp.int32, (192, 1), 0)
        packed = (st[...] * jnp.where(row < 128, 0.125, 1.0)).astype(BF16)
        home = att_rows(2 * lax.rem(s, 2) + s // 2, 0, 192)
        wdn[1 + j, home] = dot_nn(packed, tok[...]).astype(BF16)
        sums = dot_nt(jnp.ones((8, SEQ), BF16), packed)
        vec[pl.ds(12 + h, 1), 0:192] = sums[0:1]
        w_rows = wqkv[s, block(j, 192)]

        acc[...] = acc[...] + dot_tn(packed, w_rows)

        for k in range(12):
            @pl.when(n == k)
            def _():
                if k % 4 == 0:
                    run_stage(1, 6 + k // 4)
                if k % 4 == 3:
                    run_stage(0, 7 + k // 4)
                for piece, s in AFTER_HEAD.get(k, ()):
                    late_stage(piece, s)

        return carry

    lax.fori_loop(0, 12, head_back, 0)
    def vec_copy(k):
        return send(vec_acc.at[k], vec_in.at[k], vs.at[k], vr.at[k], partners[k])

    def vec_step(k):
        if k > 0:
            vec_copy(k - 1).wait()
            total = vec_acc[k - 1] + vec_in[k - 1]
            if k == len(partners):
                vec_out[...] = total
                return
            vec_acc[k] = total
        vec_copy(k).start()

    vec_step(0)
    gtok[...] = acc[...].astype(BF16)
    run_stage(1, 9)
    vec_step(1)
    tok_copies = spread(1, gtok, grad_out)
    for copy in (*tok_copies[:3], lay_copies[1]):
        copy.start()
    for piece, s in AFTER_LAST:
        if piece == -3:
            for k in (s,) if s < 5 else range(5, len(partners) + 1):
                vec_step(k)
        elif piece < 0:
            copies = tok_copies if piece == -1 else lay_copies
            copies[1].wait()
            copies[3].start()
        else:
            late_stage(piece, s)
    for copies in (lay_copies, tok_copies):
        copies[0].wait()
        copies[2].wait()
        copies[3].wait()


def run_layer(dp, tokens, cotangent, key_lengths, slot_counts, shards, rows):
    dp_bits = dp.bit_length() - 1
    n_exchange = dp_bits - 2
    stages = 4 + n_exchange + 2
    links = dp_bits + 2
    vmem = pl.BlockSpec(memory_space=pltpu.VMEM)
    smem = pl.BlockSpec(memory_space=pltpu.SMEM)
    hbm = pl.BlockSpec(memory_space=pltpu.HBM)
    dma = pltpu.SemaphoreType.DMA
    return pl.pallas_call(
        functools.partial(layer_kernel, dp_bits),
        out_shape=[
            jax.ShapeDtypeStruct((4, SEQ, D), BF16),
            jax.ShapeDtypeStruct((4, SEQ, D), BF16),
            jax.ShapeDtypeStruct((6, 2, 2, 64, D), BF16),
            jax.ShapeDtypeStruct((4, 2, 2, 48, D), BF16),
            jax.ShapeDtypeStruct((24, D), F32),
        ],
        in_specs=[hbm, hbm, smem, smem] + [hbm] * 4 + [vmem],
        out_specs=[hbm] * 2 + [vmem] * 3,
        scratch_shapes=[
            *[pltpu.VMEM((4, *s.shape), BF16) for s in shards],
            pltpu.VMEM((4, 8, D), F32),
            pltpu.VMEM((SEQ, D), BF16),
            pltpu.VMEM((SEQ, D), BF16),
            pltpu.VMEM((12, SEQ, 192), BF16),
            pltpu.VMEM((4, SEQ, 192), BF16),
            pltpu.VMEM((4, SEQ, 128), F32),
            pltpu.VMEM((SEQ, D), F32),
            pltpu.VMEM((SEQ, 1), F32),
            pltpu.VMEM((SEQ, D), BF16),
            pltpu.VMEM((4, SEQ, D), BF16),
            pltpu.VMEM((4, SEQ, D), BF16),
            pltpu.VMEM((SEQ, D), F32),
            pltpu.VMEM((SEQ, D), BF16),
            pltpu.VMEM((SEQ, D), F32),
            pltpu.VMEM((12, SEQ, 64), BF16),
            pltpu.VMEM((192, SEQ), F32),
            pltpu.VMEM((2, SEQ, D), BF16),
            pltpu.VMEM((6, 2, 2, 2, 2, 64, D), BF16),
            pltpu.VMEM((6, 2, 2, 2, 64, D), BF16),
            pltpu.VMEM((6, 2, 2, 64, D), BF16),
            pltpu.VMEM((6, 2, 64, D), BF16),
            pltpu.VMEM((6, 64, D), BF16),
            pltpu.VMEM((6, n_exchange, 64, D), BF16),
            pltpu.VMEM((4, n_exchange, 48, D), BF16),
            pltpu.VMEM((links, 24, D), F32),
            pltpu.VMEM((links, 24, D), F32),
            dma((8, 5)), dma((8, 5)),
            dma((stages, PIECES)), dma((stages, PIECES)),
            dma((links,)), dma((links,)),
            dma((2, 3)), dma((2, 3)),
            dma((3,)), dma((3,)),
            dma((8,)),
            pltpu.SemaphoreType.REGULAR,
        ],
        compiler_params=pltpu.CompilerParams(
            collective_id=0, has_side_effects=True, vmem_limit_bytes=67043328
        ),
    )(tokens, cotangent, key_lengths, slot_counts, *shards, rows)


def per_device(dp, tokens, cotangent, key_lengths, slot_counts, *params):
    (w_query, b_query, w_key, w_value, b_value, w_out, b_out, attn_gain, attn_shift,
     w_up, b_up, w_down, b_down, ffn_gain, ffn_shift) = params
    slot = lax.axis_index("tensor")
    heads = w_query.shape[1] // HD
    qkv = jnp.stack([w.reshape(D, heads, HD) for w in (w_query, w_key, w_value)], 1)
    qkv = qkv.transpose(2, 1, 3, 0).reshape(-1, D)
    q_bias = b_query.reshape(heads, HD)
    v_bias = b_value.reshape(heads, HD)
    qkv_bias = jnp.concatenate(
        (q_bias, jnp.zeros_like(q_bias), v_bias, jnp.zeros((heads, D - 3 * HD), BF16)), 1
    )
    rows = jnp.concatenate(
        [v[None] for v in (b_out, attn_gain, attn_shift, b_down, ffn_gain, ffn_shift)]
        + [jnp.zeros((2, D), BF16), b_up[None], qkv_bias, jnp.zeros((4, D), BF16)], 0
    ).astype(F32)
    layer, grad, off, oat, vec = run_layer(
        dp, tokens, cotangent, key_lengths, slot_counts, (qkv, w_out, w_up, w_down), rows
    )
    off = off.reshape(2, -1, D).astype(F32)
    oat = oat.reshape(4, -1, D)
    g_out = oat[0].astype(F32)
    g_qkv = oat[1:].reshape(heads, 3, HD, D)
    g_q, g_k, g_v = (g_qkv[:, i].reshape(-1, D).T.astype(F32) for i in range(3))
    b_qkv = lax.dynamic_slice_in_dim(vec[12:, :3 * HD], slot * heads, heads)
    gb_up = lax.dynamic_slice_in_dim(vec[8:12], slot, 1)[0]
    return (layer.reshape(-1, D), grad.reshape(-1, D),
            g_q, b_qkv[:, :HD].reshape(-1), g_k, g_v, b_qkv[:, 2 * HD:].reshape(-1), g_out,
            vec[3], vec[4], vec[5], off[1], gb_up, off[0], vec[0], vec[1], vec[2])


def solution(mesh):
    placed = (
        P("dp", None),
        P("dp", None),
        P("dp"),
        P("dp"),
        P(None, "tensor"),
        P("tensor"),
        P(None, "tensor"),
        P(None, "tensor"),
        P("tensor"),
        P("tensor", None),
        P(),
        P(),
        P(),
        P(None, "tensor"),
        P("tensor"),
        P("tensor", None),
        P(),
        P(),
        P(),
    )
    return jax.shard_map(
        functools.partial(per_device, mesh.shape["dp"]),
        mesh=mesh,
        in_specs=placed,
        out_specs=(
            P("dp", None),
            P("dp", None),
            P(None, "tensor"),
            P("tensor"),
            P(None, "tensor"),
            P(None, "tensor"),
            P("tensor"),
            P("tensor", None),
            P(),
            P(),
            P(),
            P(None, "tensor"),
            P("tensor"),
            P("tensor", None),
            P(),
            P(),
            P(),
        ),
        check_vma=False,
    )
```

```python
import functools

import jax
import jax.numpy as jnp
from jax import lax
from jax.experimental import pallas as pl
from jax.experimental.pallas import tpu as pltpu
from jax.sharding import PartitionSpec as P

D = 768
HD = 64
SEQ = 512
MESH = pl.DeviceIdType.MESH
F32 = jnp.float32
BF16 = jnp.bfloat16
FF_PIECES = 6
PIECES = 10
ORDERS = ("yxz", "yzx", "xyz", "zxy", "yzx", "xyz", "xyz", "xyz", "xyz", "xyz")
AFTER_HEAD = {
    0: ((0, 2), (2, 2), (1, 2), (3, 2)),
    1: ((4, 2),),
    3: ((5, 2),),
    4: ((2, 3), (1, 3)),
    6: ((4, 3), (5, 3), (6, 2)),
    7: ((2, 4),),
    8: ((0, 3), (5, 4)),
    9: ((6, 3), (3, 3)),
    11: ((0, 4), (2, 5)),
}
AFTER_LAST = (
    (5, 5), (6, 4), (7, 2), (1, 4), (2, 6), (0, 5), (4, 4), (5, 6),
    (7, 3), (3, 4), (2, 7), (6, 5), (8, 2), (0, 6), (5, 7), (-3, 2),
    (1, 5), (9, 2), (8, 3), (7, 4), (4, 5), (0, 7), (-3, 3), (6, 6),
    (1, 6), (8, 4), (9, 3), (3, 5), (-3, 4), (4, 6), (6, 7), (7, 5),
    (-1, 0), (1, 7), (9, 4), (8, 5), (-3, 5), (7, 6), (4, 7), (8, 6),
    (9, 5), (3, 6), (7, 7), (9, 6), (8, 7), (-2, 0), (9, 7), (3, 7),
)
VIA = (1, 0, 1, 0, 1, 1, 0, 1)
FETCH_HEAD = {(1, 2): ((0, 0),), (2, 0): ((0, 1), (0, 2)), (2, 2): ((0, 3),), (3, 1): ((1, 1),), (3, 2): ((0, 4),)}
FETCH_NORM = ((1, 2), (0, 5))
FETCH_UP = {1: ((1, 3),), 2: ((0, 6), (1, 4)), 3: ((0, 7),)}
FETCH_DOWN = {0: ((1, 5),)}


def flip(value, bit):
    return value + bit - 2 * bit * lax.rem(value // bit, 2)


def dot_nn(a, b):
    return lax.dot_general(a, b, (((1,), (0,)), ((), ())), preferred_element_type=F32)


def dot_nt(a, b):
    return lax.dot_general(a, b, (((1,), (1,)), ((), ())), preferred_element_type=F32)


def dot_tn(a, b):
    return lax.dot_general(a, b, (((0,), (0,)), ((), ())), preferred_element_type=F32)


def row_mean(value):
    return jnp.sum(value, -1, keepdims=True) * (1.0 / D)


def col_sum(value):
    return jnp.sum(value, 0, keepdims=True)


def norm_back(grad, normed, inv_std):
    return inv_std * (grad - row_mean(grad) - normed * row_mean(grad * normed))


def block(index, size):
    return pl.ds(pl.multiple_of(index * size, size), size)


def layer_kernel(dp_bits, tok_hbm, cot_hbm, len_ref, cnt_ref, qkv_own, out_own, up_own, down_own,
                 *refs):
    vectors, refs = refs[:9], refs[9:]
    (layer_out, grad_out, off_ref, oat_ref, vec_out,
                 wqkv, wo, wup, wdn, bias, tok, cot, qkv, ctx, lse, n1, r1, flow, hid, gd, gr2,
                 glow, acc, gctx, st, stage_rows, gff, r0, r1f, r2, r3, rx, rxa, vec_acc, vec_in,
                 ws, wr, gs, gr, vs, vr, os, orr, bs, br, ls, free_sem, rows_ref) = refs
    t = lax.axis_index("tensor")
    d = lax.axis_index("dp")
    c = lax.rem(t, 2)
    x = t // 2
    b0 = lax.rem(d, 2)
    b1 = lax.rem(d // 2, 2)
    other = flip(t, 2)
    core = {"tensor": flip(t, 1)}
    across = {"tensor": other}
    dps = [{"dp": flip(d, 1 << k)} for k in range(dp_bits)]
    partners = (core, across, *dps)

    def send(src, dst, send_sem, recv_sem, device):
        return pltpu.make_async_remote_copy(
            src_ref=src, dst_ref=dst, send_sem=send_sem, recv_sem=recv_sem,
            device_id=device, device_id_type=MESH,
        )

    def slot_of(order):
        oc = lax.rem(order, 2)
        ox = order // 2
        return (x + ox - 2 * x * ox) * 2 + c + oc - 2 * c * oc

    loads = [
        pltpu.make_async_copy(tok_hbm.at[block(t, SEQ)], tok, ls.at[0]),
        pltpu.make_async_copy(qkv_own, wqkv.at[t], ls.at[1]),
        pltpu.make_async_copy(out_own, wo.at[t], ls.at[2]),
        pltpu.make_async_copy(up_own, wup.at[t], ls.at[3]),
        pltpu.make_async_copy(down_own, wdn.at[t], ls.at[4]),
        pltpu.make_async_copy(cot_hbm.at[block(t, SEQ)], cot, ls.at[5]),
    ]
    for load in loads:
        load.start()
    rows_ref[...] = jnp.zeros_like(rows_ref)
    for i, ref in enumerate(vectors):
        row = i if i < 6 else i + 2
        width = ref.shape[0]
        rows_ref[row:row + 1, 0:width] = ref[...].astype(F32).reshape(1, width)
    bias[t] = rows_ref[8:16]
    barrier = pltpu.get_barrier_semaphore()
    for device in partners:
        pl.semaphore_signal(barrier, inc=1, device_id=device, device_id_type=MESH)
    pl.semaphore_wait(barrier, len(partners))

    mine8 = rows_ref.at[pl.ds(8, 8)]
    bias_hop = send(mine8, bias.at[t], bs.at[0], br.at[0], across)
    bias_chip = send(mine8, bias.at[t], bs.at[1], br.at[1], core)
    bias_mate = send(bias.at[other], bias.at[other], bs.at[2], br.at[2], core)
    bias_hop.start()
    bias_chip.start()

    half_up = up_own.shape[0] // 2
    part_down = down_own.shape[0] // 4
    chunks = [
        (qkv_own, wqkv, 0, qkv_own.shape[0]), (out_own, wo, 0, out_own.shape[0]),
        (up_own, wup, 0, half_up), (up_own, wup, half_up, half_up),
        *[(down_own, wdn, k * part_down, part_down) for k in range(4)],
    ]

    def span(base, rows, which):
        return pl.ds(pl.multiple_of(base + which * (rows // 2), 16), rows // 2)

    hops, chips, relays, mates, lasts = [], [], [], [], []
    for i, (own, full, base, rows) in enumerate(chunks):
        bit = (b0, b1)[VIA[i]]
        hops.append(send(own.at[span(base, rows, bit)], full.at[t, span(base, rows, bit)],
                         ws.at[i, 1], wr.at[i, 1], across))
        chips.append(send(own.at[pl.ds(base, rows)], full.at[t, pl.ds(base, rows)],
                          ws.at[i, 0], wr.at[i, 0], core))
        here = full.at[other, span(base, rows, bit)]
        there = full.at[other, span(base, rows, 1 - bit)]
        relays.append(send(here, here, ws.at[i, 2], wr.at[i, 2], dps[VIA[i]]))
        mates.append(send(here, here, ws.at[i, 3], wr.at[i, 3], core))
        lasts.append(send(there, there, ws.at[i, 4], wr.at[i, 4], core))
        hops[i].start()
        chips[i].start()

    def from_across(i):
        hops[i].wait()
        relays[i].start()
        mates[i].start()

    def from_beside(i):
        relays[i].wait()
        lasts[i].start()

    def fetch(steps):
        for over_dp, i in steps:
            (from_beside if over_dp else from_across)(i)

    def from_core(i):
        chips[i].wait()

    def from_far(i):
        mates[i].wait()
        lasts[i].wait()

    live = jnp.where(t < cnt_ref[0], 1.0, 0.0).astype(F32)
    length = len_ref[t]
    key_mask = jnp.where(
        lax.broadcasted_iota(jnp.int32, (1, SEQ), 1) < length, 0.0, -1e30
    ).astype(F32)
    vec_acc[0] = jnp.zeros_like(vec_acc[0])
    vec = vec_acc.at[0]

    def add_vec(row, value):
        vec[pl.ds(row, 1)] = vec[pl.ds(row, 1)] + value

    loads[0].wait()
    loads[1].wait()

    def attend(order, carry):
        s = slot_of(order)

        @pl.when(order == 1)
        def _():
            bias_hop.wait()
            bias_mate.start()
            from_core(0)
            bias_chip.wait()

        @pl.when(order == 2)
        def _():
            from_beside(0)
            bias_mate.wait()

        @pl.when(order == 3)
        def _():
            from_far(0)

        for j in range(3):
            h = 3 * s + j
            w_rows = wqkv[s, 192 * j:192 * (j + 1)]
            lanes = slice(64 * j, 64 * (j + 1))
            packed = dot_nt(tok[...], w_rows)
            qkv[h, :, 0:64] = (packed[:, 0:64] + bias[s, 1:2, lanes]).astype(BF16)
            qkv[h, :, 64:128] = packed[:, 64:128].astype(BF16)
            qkv[h, :, 128:192] = (packed[:, 128:192] + bias[s, 2:3, lanes]).astype(BF16)
            keys = qkv[h, :, 64:128]
            values = qkv[h, :, 128:192]

            def rows(rb, carry):
                at = block(rb, 512)
                scores = dot_nt(qkv[h, at, 0:64], keys) * 0.125 + key_mask
                top = jnp.max(scores, -1, keepdims=True)
                expd = jnp.exp(scores - top)
                total = jnp.sum(expd, -1, keepdims=True)
                probs = (expd * (1.0 / total)).astype(BF16)
                ctx[s, at, 64 * j:64 * (j + 1)] = dot_nn(probs, values).astype(BF16)
                lane = lax.broadcasted_iota(jnp.int32, (512, 128), 1)
                lse[s, at] = jnp.where(lane == j, top + jnp.log(total), lse[s, at])
                return carry

            lax.fori_loop(0, SEQ // 512, rows, 0, unroll=True)
            for o in range(4):
                if (o, j) in FETCH_HEAD:
                    @pl.when(order == o)
                    def _():
                        fetch(FETCH_HEAD[(o, j)])
        return carry

    lse[...] = jnp.zeros_like(lse)
    lax.fori_loop(0, 4, attend, 0)

    from_core(1)
    from_far(1)
    loads[2].wait()
    gain1 = rows_ref[1:2]
    shift1 = rows_ref[2:3]

    def project(rb, carry):
        at = block(rb, 128)
        total = tok[at].astype(F32) + rows_ref[0:1]
        for s in range(4):
            total = total + dot_nn(ctx[s, at], wo[s])
        center = total - row_mean(total)
        inv = lax.rsqrt(row_mean(center * center) + 1e-5)
        normed = center * inv
        out = normed * gain1 + shift1
        n1[at] = normed
        r1[at] = inv
        flow[at] = out.astype(BF16)
        acc[at] = out + rows_ref[3:4]
        return carry

    lax.fori_loop(0, 4, project, 0)

    fetch(FETCH_NORM)
    loads[3].wait()

    def raise_up(order, carry):
        s = slot_of(order)

        @pl.when(order == 1)
        def _():
            from_core(2)
            from_core(3)

        @pl.when(order == 3)
        def _():
            from_far(2)
            from_far(3)

        def rows(rb, carry):
            at = block(rb, 128)
            pre = dot_nn(flow[at], wup[s]) + bias[s, 0:1]
            cdf = 0.5 + 0.5 * lax.erf(pre * 0.7071067811865476)
            pdf = jnp.exp(pre * pre * -0.5) * 0.3989422804014327
            hid[s, at] = (pre * cdf).astype(BF16)
            gd[s, at] = (cdf + pre * pdf).astype(BF16)
            return carry

        lax.fori_loop(0, 4, rows, 0)
        for o, steps in FETCH_UP.items():
            @pl.when(order == o)
            def _():
                fetch(steps)
        return carry

    lax.fori_loop(0, 4, raise_up, 0)
    loads[4].wait()

    def bring_down(order, carry):
        s = slot_of(order)

        @pl.when(order == 1)
        def _():
            for i in range(4, 8):
                from_core(i)

        @pl.when(order == 2)
        def _():
            from_beside(6)
            from_beside(7)

        @pl.when(order == 3)
        def _():
            for i in range(4, 8):
                from_far(i)

        def rows(rb, carry):
            at = block(rb, 256)
            acc[at] = acc[at] + dot_nn(hid[s, at], wdn[s])
            return carry

        lax.fori_loop(0, 2, rows, 0)
        for o, steps in FETCH_DOWN.items():
            @pl.when(order == o)
            def _():
                fetch(steps)
        return carry

    lax.fori_loop(0, 4, bring_down, 0)

    loads[5].wait()
    gain2 = rows_ref[4:5]
    shift2 = rows_ref[5:6]
    lay = stage_rows.at[0]
    gtok = stage_rows.at[1]

    def second(rb, carry):
        at = block(rb, 128)
        total = acc[at]
        center = total - row_mean(total)
        inv = lax.rsqrt(row_mean(center * center) + 1e-5)
        normed = center * inv
        lay[at] = (live * (normed * gain2 + shift2)).astype(BF16)
        grad = live * cot[at].astype(F32)
        add_vec(1, col_sum(grad * normed))
        add_vec(2, col_sum(grad))
        back = norm_back(grad * gain2, normed, inv)
        low = back.astype(BF16)
        gr2[at] = back
        glow[at] = low
        add_vec(0, col_sum(low.astype(F32)))
        acc[at] = jnp.zeros_like(total)
        return carry

    lax.fori_loop(0, 4, second, 0)

    def spread(i, src, dst):
        return (
            pltpu.make_async_copy(src, dst.at[t], ls.at[6 + i]),
            send(src, dst.at[t], os.at[i, 0], orr.at[i, 0], across),
            send(src, dst.at[t], os.at[i, 1], orr.at[i, 1], core),
            send(dst.at[other], dst.at[other], os.at[i, 2], orr.at[i, 2], core),
        )

    lay_copies = spread(0, lay, layer_out)
    lay_copies[0].start()
    lay_copies[2].start()

    n_exchange = dp_bits - 2
    last = 4 + n_exchange + 2

    def att_rows(shard, quarter, count):
        return pl.ds(pl.multiple_of((shard * 4 + quarter) * 48, 48), count)

    mine = {"x": x, "y": b0, "z": b1}
    peer = {"x": across, "y": dps[0], "z": dps[1]}
    got_ff = (r0, r1f, r2, r3)
    all_rows = slice(None)

    def halves(piece, s):
        if piece < FF_PIECES:
            place = {axis: mine[axis] for axis in ORDERS[piece][:max(s - 1, 0)]}
            at = [piece, c] + [place.get(axis, all_rows) for axis in "xyz"]
            away, keep = list(at), list(at)
            if s == 0:
                away[1] = 1 - c
            else:
                axis = ORDERS[piece][s - 1]
                away["xyz".index(axis) + 2] = 1 - mine[axis]
                keep["xyz".index(axis) + 2] = mine[axis]
            return gff.at[tuple(away)], gff.at[tuple(keep)], got_ff[s].at[piece]
        g = wdn.at[piece - FF_PIECES]
        r = wup.at[piece - FF_PIECES]
        me = 2 * c + x
        if s == 0:
            return g.at[att_rows(2 * (1 - c), 0, 384)], g.at[att_rows(2 * c, 0, 384)], r.at[pl.ds(0, 384)]
        if s == 1:
            return g.at[att_rows(2 * c + 1 - x, 0, 192)], g.at[att_rows(me, 0, 192)], r.at[pl.ds(384, 192)]
        if s == 2:
            return (g.at[att_rows(me, 2 * (1 - b0), 96)], g.at[att_rows(me, 2 * b0, 96)],
                    r.at[pl.ds(576, 96)])
        return (g.at[att_rows(me, 2 * b0 + 1 - b1, 48)], g.at[att_rows(me, 2 * b0 + b1, 48)],
                r.at[pl.ds(672, 48)])

    def kept(piece):
        if piece < FF_PIECES:
            return gff.at[piece, c, x, b0, b1], rx.at[piece], off_ref.at[piece]
        own = wdn.at[piece - FF_PIECES, att_rows(2 * c + x, 2 * b0 + b1, 48)]
        return own, rxa.at[piece - FF_PIECES], oat_ref.at[piece - FF_PIECES]

    def stage_copy(s, piece):
        sems = (gs.at[s, piece], gr.at[s, piece])
        order = ORDERS[piece]
        if s < 4:
            away, _, got = halves(piece, s)
            return send(away, got, *sems, core if s == 0 else peer[order[s - 1]])
        own, got, out = kept(piece)
        if s < 4 + n_exchange:
            return send(own, got.at[s - 4], *sems, dps[s - 2])
        back = [axis for axis in order if axis != "x"]
        if s == 4 + n_exchange:
            part = out.at[b0, b1]
            return send(part, part, *sems, peer[back[1]])
        part = out.at[b0] if back[0] == "y" else out.at[:, b1]
        return send(part, part, *sems, peer[back[0]])

    def combine(s, piece):
        if s < 4:
            _, keep, got = halves(piece, s)
            keep[...] = keep[...] + got[...]
        elif s < 4 + n_exchange:
            own, got, out = kept(piece)
            total = own[...] + got[s - 4]
            if s == 3 + n_exchange:
                out[b0, b1] = total
            else:
                own[...] = total

    def run_stage(s, piece):
        if s > 0:
            stage_copy(s - 1, piece).wait()
            combine(s - 1, piece)
        if s < last:
            stage_copy(s, piece).start()

    def late_stage(piece, s):
        if s < 5:
            run_stage(s, piece)
        elif s == 5:
            for k in range(5, 5 + n_exchange):
                run_stage(k, piece)
        else:
            run_stage(s + n_exchange - 1, piece)

    def down_grad(i, carry):
        def shard(s, carry):
            value = dot_tn(hid[s, :, block(i, 256)], glow[...]).astype(BF16)
            for q in range(4):
                gff[i, lax.rem(s, 2), s // 2, q // 2, q % 2] = value[64 * q:64 * (q + 1)]
            return carry

        lax.fori_loop(0, 4, shard, 0)
        for k in range(3):
            @pl.when(i == k)
            def _():
                run_stage(0, k)
                if k > 0:
                    run_stage(1, k - 1)

        return carry

    lax.fori_loop(0, 3, down_grad, 0)

    def ffn_back(s, carry):
        @pl.when(s == 1)
        def _():
            run_stage(1, 2)

        def rows(rb, carry):
            at = block(rb, 256)
            low = (dot_nt(glow[at], wdn[s]) * gd[s, at].astype(F32)).astype(BF16)
            gd[s, at] = low
            add_vec(8 + s, col_sum(low.astype(F32)))
            acc[at] = acc[at] + dot_nt(low, wup[s])
            return carry

        lax.fori_loop(0, 2, rows, 0)
        return carry

    lax.fori_loop(0, 4, ffn_back, 0)
    for device in partners:
        pl.semaphore_signal(free_sem, inc=1, device_id=device, device_id_type=MESH)

    def up_grad(i, carry):
        def shard(s, carry):
            value = dot_tn(flow[:, block(i, 256)], gd[s]).astype(BF16)
            for q in range(4):
                gff[3 + i, lax.rem(s, 2), s // 2, q // 2, q % 2] = value[64 * q:64 * (q + 1)]
            return carry

        lax.fori_loop(0, 4, shard, 0)
        for k in range(3):
            @pl.when(i == k)
            def _():
                run_stage(0, 3 + k)
                if k > 0:
                    run_stage(1, 2 + k)

        return carry

    lax.fori_loop(0, 3, up_grad, 0)

    def first_back(rb, carry):
        at = block(rb, 128)
        grad = gr2[at] + acc[at]
        normed = n1[at]
        add_vec(4, col_sum(grad * normed))
        add_vec(5, col_sum(grad))
        back = norm_back(grad * gain1, normed, r1[at])
        low = back.astype(BF16)
        acc[at] = back
        glow[at] = low
        add_vec(3, col_sum(low.astype(F32)))
        return carry

    lax.fori_loop(0, 4, first_back, 0)
    run_stage(1, 5)

    pl.semaphore_wait(free_sem, len(partners))

    def out_back(s, carry):
        home = att_rows(2 * lax.rem(s, 2) + s // 2, 0, 192)
        wdn[0, home] = dot_tn(ctx[s], glow[...]).astype(BF16)
        back = dot_nt(glow[...], wo[s]).astype(BF16)
        for j in range(3):
            gctx[3 * s + j] = back[:, 64 * j:64 * (j + 1)]
        return carry

    lax.fori_loop(0, 4, out_back, 0)
    run_stage(0, 6)

    def head_back(n, carry):
        s = slot_of(lax.rem(n, 4))
        j = n // 4
        h = 3 * s + j
        keys = qkv[h, :, 64:128]
        values = qkv[h, :, 128:192]
        keys_t = keys.T
        st[...] = jnp.zeros_like(st)

        def rows(rb, carry):
            at = block(rb, 512)
            query = qkv[h, at, 0:64]
            gout = gctx[h, at]
            lane = lax.broadcasted_iota(jnp.int32, (512, 128), 1)
            norm = jnp.sum(jnp.where(lane == j, lse[s, at], 0.0), -1, keepdims=True)
            probs = jnp.exp(dot_nt(query, keys) * 0.125 + key_mask - norm)
            gprobs = dot_nt(gout, values)
            scored = probs * (gprobs - jnp.sum(gprobs * probs, -1, keepdims=True))
            scored = scored.astype(BF16)
            st[0:64, at] = dot_nt(keys_t, scored)
            st[64:128] = st[64:128] + dot_tn(query, scored)
            st[128:192] = st[128:192] + dot_tn(gout, probs.astype(BF16))
            return carry

        lax.fori_loop(0, SEQ // 512, rows, 0, unroll=True)
        row = lax.broadcasted_iota(jnp.int32, (192, 1), 0)
        packed = (st[...] * jnp.where(row < 128, 0.125, 1.0)).astype(BF16)
        home = att_rows(2 * lax.rem(s, 2) + s // 2, 0, 192)
        wdn[1 + j, home] = dot_nn(packed, tok[...]).astype(BF16)
        sums = dot_nt(jnp.ones((8, SEQ), BF16), packed)
        vec[pl.ds(12 + h, 1), 0:192] = sums[0:1]
        w_rows = wqkv[s, block(j, 192)]

        acc[...] = acc[...] + dot_tn(packed, w_rows)

        for k in range(12):
            @pl.when(n == k)
            def _():
                if k % 4 == 0:
                    run_stage(1, 6 + k // 4)
                if k % 4 == 3:
                    run_stage(0, 7 + k // 4)
                for piece, s in AFTER_HEAD.get(k, ()):
                    late_stage(piece, s)

        return carry

    lax.fori_loop(0, 12, head_back, 0)
    def vec_copy(k):
        return send(vec_acc.at[k], vec_in.at[k], vs.at[k], vr.at[k], partners[k])

    def vec_step(k):
        if k > 0:
            vec_copy(k - 1).wait()
            total = vec_acc[k - 1] + vec_in[k - 1]
            if k == len(partners):
                vec_out[...] = total
                return
            vec_acc[k] = total
        vec_copy(k).start()

    vec_step(0)
    gtok[...] = acc[...].astype(BF16)
    run_stage(1, 9)
    vec_step(1)
    tok_copies = spread(1, gtok, grad_out)
    for copy in (*tok_copies[:3], lay_copies[1]):
        copy.start()
    for piece, s in AFTER_LAST:
        if piece == -3:
            for k in (s,) if s < 5 else range(5, len(partners) + 1):
                vec_step(k)
        elif piece < 0:
            copies = tok_copies if piece == -1 else lay_copies
            copies[1].wait()
            copies[3].start()
        else:
            late_stage(piece, s)
    for copies in (lay_copies, tok_copies):
        copies[0].wait()
        copies[2].wait()
        copies[3].wait()


def run_layer(dp, tokens, cotangent, key_lengths, slot_counts, shards, vectors):
    dp_bits = dp.bit_length() - 1
    n_exchange = dp_bits - 2
    stages = 4 + n_exchange + 2
    links = dp_bits + 2
    vmem = pl.BlockSpec(memory_space=pltpu.VMEM)
    smem = pl.BlockSpec(memory_space=pltpu.SMEM)
    hbm = pl.BlockSpec(memory_space=pltpu.HBM)
    dma = pltpu.SemaphoreType.DMA
    return pl.pallas_call(
        functools.partial(layer_kernel, dp_bits),
        out_shape=[
            jax.ShapeDtypeStruct((4, SEQ, D), BF16),
            jax.ShapeDtypeStruct((4, SEQ, D), BF16),
            jax.ShapeDtypeStruct((6, 2, 2, 64, D), BF16),
            jax.ShapeDtypeStruct((4, 2, 2, 48, D), BF16),
            jax.ShapeDtypeStruct((24, D), F32),
        ],
        in_specs=[hbm, hbm, smem, smem] + [hbm] * 4 + [vmem] * len(vectors),
        out_specs=[hbm] * 2 + [vmem] * 3,
        scratch_shapes=[
            *[pltpu.VMEM((4, *s.shape), BF16) for s in shards],
            pltpu.VMEM((4, 8, D), F32),
            pltpu.VMEM((SEQ, D), BF16),
            pltpu.VMEM((SEQ, D), BF16),
            pltpu.VMEM((12, SEQ, 192), BF16),
            pltpu.VMEM((4, SEQ, 192), BF16),
            pltpu.VMEM((4, SEQ, 128), F32),
            pltpu.VMEM((SEQ, D), F32),
            pltpu.VMEM((SEQ, 1), F32),
            pltpu.VMEM((SEQ, D), BF16),
            pltpu.VMEM((4, SEQ, D), BF16),
            pltpu.VMEM((4, SEQ, D), BF16),
            pltpu.VMEM((SEQ, D), F32),
            pltpu.VMEM((SEQ, D), BF16),
            pltpu.VMEM((SEQ, D), F32),
            pltpu.VMEM((12, SEQ, 64), BF16),
            pltpu.VMEM((192, SEQ), F32),
            pltpu.VMEM((2, SEQ, D), BF16),
            pltpu.VMEM((6, 2, 2, 2, 2, 64, D), BF16),
            pltpu.VMEM((6, 2, 2, 2, 64, D), BF16),
            pltpu.VMEM((6, 2, 2, 64, D), BF16),
            pltpu.VMEM((6, 2, 64, D), BF16),
            pltpu.VMEM((6, 64, D), BF16),
            pltpu.VMEM((6, n_exchange, 64, D), BF16),
            pltpu.VMEM((4, n_exchange, 48, D), BF16),
            pltpu.VMEM((links, 24, D), F32),
            pltpu.VMEM((links, 24, D), F32),
            dma((8, 5)), dma((8, 5)),
            dma((stages, PIECES)), dma((stages, PIECES)),
            dma((links,)), dma((links,)),
            dma((2, 3)), dma((2, 3)),
            dma((3,)), dma((3,)),
            dma((8,)),
            pltpu.SemaphoreType.REGULAR,
            pltpu.VMEM((16, D), F32),
        ],
        compiler_params=pltpu.CompilerParams(
            collective_id=0, has_side_effects=True, vmem_limit_bytes=67043328
        ),
    )(tokens, cotangent, key_lengths, slot_counts, *shards, *vectors)


def finish_kernel(layer, grad, ff, att, vec, layer_out, grad_out, down, up, out, g_q, g_k, g_v, *sums):
    layer_out[...] = layer[0]
    grad_out[...] = grad[0]
    down[...] = ff[0].astype(F32)
    up[...] = ff[1].astype(F32)

    @pl.when(pl.program_id(0) == 0)
    def _():
        t = lax.axis_index("tensor")
        out[...] = att[0].astype(F32)
        for i, ref in enumerate((g_q, g_k, g_v)):
            for j in range(3):
                ref[64 * j:64 * (j + 1)] = att[1 + j, 64 * i:64 * (i + 1)].astype(F32)
        for i, ref in enumerate(sums):
            row = vec[i:i + 1] if i < 6 else vec[pl.ds(8 + t, 1)]
            ref[...] = row.reshape(D)


def finish(layer, grad, ff, att, vec):
    rows, part = 4 * SEQ, ff.shape[1] // 4
    shard = jax.ShapeDtypeStruct(att.shape[1:], F32)
    square = jax.ShapeDtypeStruct(ff.shape[1:], F32)
    line = jax.ShapeDtypeStruct((D,), F32)
    slot_in = pl.BlockSpec((1, SEQ, D), lambda i: (i, 0, 0))
    slot_out = pl.BlockSpec((SEQ, D), lambda i: (i, 0))
    part_out = pl.BlockSpec((part, D), lambda i: (i, 0))
    return pl.pallas_call(
        finish_kernel,
        grid=(4,),
        out_shape=[jax.ShapeDtypeStruct((rows, D), BF16)] * 2 + [square] * 2 + [shard] * 4 + [line] * 7,
        in_specs=[slot_in, slot_in, pl.BlockSpec((2, part, D), lambda i: (0, i, 0)),
                  pl.BlockSpec(att.shape, lambda i: (0, 0, 0)), pl.BlockSpec(vec.shape, lambda i: (0, 0))],
        out_specs=[slot_out, slot_out, part_out, part_out]
        + [pl.BlockSpec(shard.shape, lambda i: (0, 0))] * 4
        + [pl.BlockSpec((D,), lambda i: (0,))] * 7,
        compiler_params=pltpu.CompilerParams(vmem_limit_bytes=67043328),
    )(layer, grad, ff, att, vec)


def per_device(dp, tokens, cotangent, key_lengths, slot_counts, *params):
    (w_query, b_query, w_key, w_value, b_value, w_out, b_out, attn_gain, attn_shift,
     w_up, b_up, w_down, b_down, ffn_gain, ffn_shift) = params
    slot = lax.axis_index("tensor")
    heads = w_query.shape[1] // HD
    qkv = jnp.stack([w.reshape(D, heads, HD) for w in (w_query, w_key, w_value)], 1)
    qkv = qkv.transpose(2, 1, 3, 0).reshape(-1, D)
    vectors = (b_out, attn_gain, attn_shift, b_down, ffn_gain, ffn_shift, b_up, b_query, b_value)
    layer, grad, off, oat, vec = run_layer(
        dp, tokens, cotangent, key_lengths, slot_counts, (qkv, w_out, w_up, w_down), vectors
    )
    layer, grad, g_down, g_up, g_out, g_q, g_k, g_v, *sums = finish(
        layer, grad, off.reshape(2, -1, D), oat.reshape(4, -1, D), vec
    )
    b_qkv = lax.dynamic_slice_in_dim(vec[12:, :3 * HD], slot * heads, heads)
    return (layer, grad, g_q.T, b_qkv[:, :HD].reshape(-1), g_k.T, g_v.T,
            b_qkv[:, 2 * HD:].reshape(-1), g_out, sums[3], sums[4], sums[5], g_up, sums[6],
            g_down, sums[0], sums[1], sums[2])


def solution(mesh):
    placed = (
        P("dp", None),
        P("dp", None),
        P("dp"),
        P("dp"),
        P(None, "tensor"),
        P("tensor"),
        P(None, "tensor"),
        P(None, "tensor"),
        P("tensor"),
        P("tensor", None),
        P(),
        P(),
        P(),
        P(None, "tensor"),
        P("tensor"),
        P("tensor", None),
        P(),
        P(),
        P(),
    )
    return jax.shard_map(
        functools.partial(per_device, mesh.shape["dp"]),
        mesh=mesh,
        in_specs=placed,
        out_specs=(
            P("dp", None),
            P("dp", None),
            P(None, "tensor"),
            P("tensor"),
            P(None, "tensor"),
            P(None, "tensor"),
            P("tensor"),
            P("tensor", None),
            P(),
            P(),
            P(),
            P(None, "tensor"),
            P("tensor"),
            P("tensor", None),
            P(),
            P(),
            P(),
        ),
        check_vma=False,
    )
```

```python
import functools

import jax
import jax.numpy as jnp
from jax import lax
from jax.experimental import pallas as pl
from jax.experimental.pallas import tpu as pltpu
from jax.sharding import PartitionSpec as P

D = 768
HD = 64
SEQ = 512
MESH = pl.DeviceIdType.MESH
F32 = jnp.float32
BF16 = jnp.bfloat16
FF_PIECES = 6
PIECES = 10
ORDERS = ("xyz", "yxz", "zxy", "xyz", "zyx", "yzx", "xyz", "xyz", "xyz", "xyz")
AFTER_HEAD = {
    0: ((1, 2), (3, 2), (0, 2), (2, 2)),
    1: ((4, 2),),
    3: ((5, 2),),
    4: ((6, 2), (3, 3)),
    6: ((1, 3), (5, 3)),
    7: ((3, 4), (0, 3)),
    8: ((1, 4), (4, 3), (2, 3)),
    10: ((6, 3), (0, 4)),
    11: ((3, 5), (7, 2), (2, 4)),
}
AFTER_LAST = (
    (3, 6), (1, 5), (6, 4), (5, 4), (3, 7), (1, 6), (0, 5), (4, 4),
    (7, 3), (8, 2), (6, 5), (-3, 2), (9, 2), (1, 7), (0, 6), (5, 5),
    (-3, 3), (6, 6), (4, 5), (7, 4), (8, 3), (-3, 4), (9, 3), (5, 6),
    (2, 5), (0, 7), (8, 4), (7, 5), (-3, 5), (-1, 0), (6, 7), (9, 4),
    (4, 6), (7, 6), (8, 5), (5, 7), (9, 5), (4, 7), (8, 6), (7, 7),
    (9, 6), (2, 6), (8, 7), (-2, 0), (9, 7), (2, 7),
)
VIA = (1, 0, 1, 0, 1, 1, 0, 1)
FETCH_HEAD = {(1, 2): ((0, 0),), (2, 0): ((0, 1), (0, 2)), (2, 2): ((0, 3),), (3, 1): ((1, 1),), (3, 2): ((0, 4),)}
FETCH_NORM = ((1, 2), (0, 5))
FETCH_UP = {1: ((1, 3),), 2: ((0, 6), (1, 4)), 3: ((0, 7),)}
FETCH_DOWN = {0: ((1, 5),)}


def flip(value, bit):
    return value + bit - 2 * bit * lax.rem(value // bit, 2)


def dot_nn(a, b):
    return lax.dot_general(a, b, (((1,), (0,)), ((), ())), preferred_element_type=F32)


def dot_nt(a, b):
    return lax.dot_general(a, b, (((1,), (1,)), ((), ())), preferred_element_type=F32)


def dot_tn(a, b):
    return lax.dot_general(a, b, (((0,), (0,)), ((), ())), preferred_element_type=F32)


def row_mean(value):
    return jnp.sum(value, -1, keepdims=True) * (1.0 / D)


def col_sum(value):
    return jnp.sum(value, 0, keepdims=True)


def norm_back(grad, normed, inv_std):
    return inv_std * (grad - row_mean(grad) - normed * row_mean(grad * normed))


def block(index, size):
    return pl.ds(pl.multiple_of(index * size, size), size)


def layer_kernel(dp_bits, tok_hbm, cot_hbm, len_ref, cnt_ref, qkv_own, out_own, up_own, down_own,
                 *refs):
    vectors, refs = refs[:9], refs[9:]
    (layer_out, grad_out, off_ref, oat_ref, vec_out,
                 wqkv, wo, wup, wdn, bias, tok, cot, qkv, ctx, lse, n1, r1, flow, hid, gd, gr2,
                 glow, acc, gctx, st, stage_rows, gff, r0, r1f, r2, r3, rx, rxa, vec_acc, vec_in,
                 ws, wr, gs, gr, vs, vr, os, orr, bs, br, ls, free_sem, rows_ref) = refs
    t = lax.axis_index("tensor")
    d = lax.axis_index("dp")
    c = lax.rem(t, 2)
    x = t // 2
    b0 = lax.rem(d, 2)
    b1 = lax.rem(d // 2, 2)
    other = flip(t, 2)
    core = {"tensor": flip(t, 1)}
    across = {"tensor": other}
    dps = [{"dp": flip(d, 1 << k)} for k in range(dp_bits)]
    partners = (core, across, *dps)

    def send(src, dst, send_sem, recv_sem, device):
        return pltpu.make_async_remote_copy(
            src_ref=src, dst_ref=dst, send_sem=send_sem, recv_sem=recv_sem,
            device_id=device, device_id_type=MESH,
        )

    def slot_of(order):
        oc = lax.rem(order, 2)
        ox = order // 2
        return (x + ox - 2 * x * ox) * 2 + c + oc - 2 * c * oc

    loads = [
        pltpu.make_async_copy(tok_hbm.at[block(t, SEQ)], tok, ls.at[0]),
        pltpu.make_async_copy(qkv_own, wqkv.at[t], ls.at[1]),
        pltpu.make_async_copy(out_own, wo.at[t], ls.at[2]),
        pltpu.make_async_copy(up_own, wup.at[t], ls.at[3]),
        pltpu.make_async_copy(down_own, wdn.at[t], ls.at[4]),
        pltpu.make_async_copy(cot_hbm.at[block(t, SEQ)], cot, ls.at[5]),
    ]
    for load in loads:
        load.start()
    rows_ref[...] = jnp.zeros_like(rows_ref)
    for i, ref in enumerate(vectors):
        row = i if i < 6 else i + 2
        width = ref.shape[0]
        rows_ref[row:row + 1, 0:width] = ref[...].astype(F32).reshape(1, width)
    bias[t] = rows_ref[8:16]
    barrier = pltpu.get_barrier_semaphore()
    for device in partners:
        pl.semaphore_signal(barrier, inc=1, device_id=device, device_id_type=MESH)
    pl.semaphore_wait(barrier, len(partners))

    mine8 = rows_ref.at[pl.ds(8, 8)]
    bias_hop = send(mine8, bias.at[t], bs.at[0], br.at[0], across)
    bias_chip = send(mine8, bias.at[t], bs.at[1], br.at[1], core)
    bias_mate = send(bias.at[other], bias.at[other], bs.at[2], br.at[2], core)
    bias_hop.start()
    bias_chip.start()

    half_up = up_own.shape[0] // 2
    part_down = down_own.shape[0] // 4
    chunks = [
        (qkv_own, wqkv, 0, qkv_own.shape[0]), (out_own, wo, 0, out_own.shape[0]),
        (up_own, wup, 0, half_up), (up_own, wup, half_up, half_up),
        *[(down_own, wdn, k * part_down, part_down) for k in range(4)],
    ]

    def span(base, rows, which):
        return pl.ds(pl.multiple_of(base + which * (rows // 2), 16), rows // 2)

    hops, chips, relays, mates, lasts = [], [], [], [], []
    for i, (own, full, base, rows) in enumerate(chunks):
        bit = (b0, b1)[VIA[i]]
        hops.append(send(own.at[span(base, rows, bit)], full.at[t, span(base, rows, bit)],
                         ws.at[i, 1], wr.at[i, 1], across))
        chips.append(send(own.at[pl.ds(base, rows)], full.at[t, pl.ds(base, rows)],
                          ws.at[i, 0], wr.at[i, 0], core))
        here = full.at[other, span(base, rows, bit)]
        there = full.at[other, span(base, rows, 1 - bit)]
        relays.append(send(here, here, ws.at[i, 2], wr.at[i, 2], dps[VIA[i]]))
        mates.append(send(here, here, ws.at[i, 3], wr.at[i, 3], core))
        lasts.append(send(there, there, ws.at[i, 4], wr.at[i, 4], core))
        hops[i].start()
        chips[i].start()

    def from_across(i):
        hops[i].wait()
        relays[i].start()
        mates[i].start()

    def from_beside(i):
        relays[i].wait()
        lasts[i].start()

    def fetch(steps):
        for over_dp, i in steps:
            (from_beside if over_dp else from_across)(i)

    def from_core(i):
        chips[i].wait()

    def from_far(i):
        mates[i].wait()
        lasts[i].wait()

    live = jnp.where(t < cnt_ref[0], 1.0, 0.0).astype(F32)
    length = len_ref[t]
    key_mask = jnp.where(
        lax.broadcasted_iota(jnp.int32, (1, SEQ), 1) < length, 0.0, -1e30
    ).astype(F32)
    vec_acc[0] = jnp.zeros_like(vec_acc[0])
    vec = vec_acc.at[0]

    def add_vec(row, value):
        vec[pl.ds(row, 1)] = vec[pl.ds(row, 1)] + value

    loads[0].wait()
    loads[1].wait()

    def attend(order, carry):
        s = slot_of(order)

        @pl.when(order == 1)
        def _():
            bias_hop.wait()
            bias_mate.start()
            from_core(0)
            bias_chip.wait()

        @pl.when(order == 2)
        def _():
            from_beside(0)
            bias_mate.wait()

        @pl.when(order == 3)
        def _():
            from_far(0)

        for j in range(3):
            h = 3 * s + j
            w_rows = wqkv[s, 192 * j:192 * (j + 1)]
            lanes = slice(64 * j, 64 * (j + 1))
            packed = dot_nt(tok[...], w_rows)
            qkv[h, :, 0:64] = (packed[:, 0:64] + bias[s, 1:2, lanes]).astype(BF16)
            qkv[h, :, 64:128] = packed[:, 64:128].astype(BF16)
            qkv[h, :, 128:192] = (packed[:, 128:192] + bias[s, 2:3, lanes]).astype(BF16)
            keys = qkv[h, :, 64:128]
            values = qkv[h, :, 128:192]

            def rows(rb, carry):
                at = block(rb, 512)
                scores = dot_nt(qkv[h, at, 0:64], keys) * 0.125 + key_mask
                top = jnp.max(scores, -1, keepdims=True)
                expd = jnp.exp(scores - top)
                total = jnp.sum(expd, -1, keepdims=True)
                probs = (expd * (1.0 / total)).astype(BF16)
                ctx[s, at, 64 * j:64 * (j + 1)] = dot_nn(probs, values).astype(BF16)
                lane = lax.broadcasted_iota(jnp.int32, (512, 128), 1)
                lse[s, at] = jnp.where(lane == j, top + jnp.log(total), lse[s, at])
                return carry

            lax.fori_loop(0, SEQ // 512, rows, 0, unroll=True)
            for o in range(4):
                if (o, j) in FETCH_HEAD:
                    @pl.when(order == o)
                    def _():
                        fetch(FETCH_HEAD[(o, j)])
        return carry

    lse[...] = jnp.zeros_like(lse)
    lax.fori_loop(0, 4, attend, 0)

    from_core(1)
    from_far(1)
    loads[2].wait()
    gain1 = rows_ref[1:2]
    shift1 = rows_ref[2:3]

    def project(rb, carry):
        at = block(rb, 128)
        total = tok[at].astype(F32) + rows_ref[0:1]
        for s in range(4):
            total = total + dot_nn(ctx[s, at], wo[s])
        center = total - row_mean(total)
        inv = lax.rsqrt(row_mean(center * center) + 1e-5)
        normed = center * inv
        out = normed * gain1 + shift1
        n1[at] = normed
        r1[at] = inv
        flow[at] = out.astype(BF16)
        acc[at] = out + rows_ref[3:4]
        return carry

    lax.fori_loop(0, 4, project, 0)

    fetch(FETCH_NORM)
    loads[3].wait()

    def raise_up(order, carry):
        s = slot_of(order)

        @pl.when(order == 1)
        def _():
            from_core(2)
            from_core(3)

        @pl.when(order == 3)
        def _():
            from_far(2)
            from_far(3)

        def rows(rb, carry):
            at = block(rb, 128)
            pre = dot_nn(flow[at], wup[s]) + bias[s, 0:1]
            cdf = 0.5 + 0.5 * lax.erf(pre * 0.7071067811865476)
            pdf = jnp.exp(pre * pre * -0.5) * 0.3989422804014327
            hid[s, at] = (pre * cdf).astype(BF16)
            gd[s, at] = (cdf + pre * pdf).astype(BF16)
            return carry

        lax.fori_loop(0, 4, rows, 0)
        for o, steps in FETCH_UP.items():
            @pl.when(order == o)
            def _():
                fetch(steps)
        return carry

    lax.fori_loop(0, 4, raise_up, 0)
    loads[4].wait()

    def bring_down(order, carry):
        s = slot_of(order)

        @pl.when(order == 1)
        def _():
            for i in range(4, 8):
                from_core(i)

        @pl.when(order == 2)
        def _():
            from_beside(6)
            from_beside(7)

        @pl.when(order == 3)
        def _():
            for i in range(4, 8):
                from_far(i)

        def rows(rb, carry):
            at = block(rb, 256)
            acc[at] = acc[at] + dot_nn(hid[s, at], wdn[s])
            return carry

        lax.fori_loop(0, 2, rows, 0)
        for o, steps in FETCH_DOWN.items():
            @pl.when(order == o)
            def _():
                fetch(steps)
        return carry

    lax.fori_loop(0, 4, bring_down, 0)

    loads[5].wait()
    gain2 = rows_ref[4:5]
    shift2 = rows_ref[5:6]
    lay = stage_rows.at[0]
    gtok = stage_rows.at[1]

    def second(rb, carry):
        at = block(rb, 128)
        total = acc[at]
        center = total - row_mean(total)
        inv = lax.rsqrt(row_mean(center * center) + 1e-5)
        normed = center * inv
        lay[at] = (live * (normed * gain2 + shift2)).astype(BF16)
        grad = live * cot[at].astype(F32)
        add_vec(1, col_sum(grad * normed))
        add_vec(2, col_sum(grad))
        back = norm_back(grad * gain2, normed, inv)
        low = back.astype(BF16)
        gr2[at] = back
        glow[at] = low
        add_vec(0, col_sum(low.astype(F32)))
        acc[at] = jnp.zeros_like(total)
        return carry

    lax.fori_loop(0, 4, second, 0)

    def spread(i, src, dst):
        return (
            pltpu.make_async_copy(src, dst.at[t], ls.at[6 + i]),
            send(src, dst.at[t], os.at[i, 0], orr.at[i, 0], across),
            send(src, dst.at[t], os.at[i, 1], orr.at[i, 1], core),
            send(dst.at[other], dst.at[other], os.at[i, 2], orr.at[i, 2], core),
        )

    lay_copies = spread(0, lay, layer_out)
    lay_copies[0].start()
    lay_copies[2].start()

    n_exchange = dp_bits - 2
    last = 4 + n_exchange + 2

    def att_rows(shard, quarter, count):
        return pl.ds(pl.multiple_of((shard * 4 + quarter) * 48, 48), count)

    mine = {"x": x, "y": b0, "z": b1}
    peer = {"x": across, "y": dps[0], "z": dps[1]}
    got_ff = (r0, r1f, r2, r3)
    all_rows = slice(None)

    def halves(piece, s):
        if piece < FF_PIECES:
            place = {axis: mine[axis] for axis in ORDERS[piece][:max(s - 1, 0)]}
            at = [piece, c] + [place.get(axis, all_rows) for axis in "xyz"]
            away, keep = list(at), list(at)
            if s == 0:
                away[1] = 1 - c
            else:
                axis = ORDERS[piece][s - 1]
                away["xyz".index(axis) + 2] = 1 - mine[axis]
                keep["xyz".index(axis) + 2] = mine[axis]
            return gff.at[tuple(away)], gff.at[tuple(keep)], got_ff[s].at[piece]
        g = wdn.at[piece - FF_PIECES]
        r = wup.at[piece - FF_PIECES]
        me = 2 * c + x
        if s == 0:
            return g.at[att_rows(2 * (1 - c), 0, 384)], g.at[att_rows(2 * c, 0, 384)], r.at[pl.ds(0, 384)]
        if s == 1:
            return g.at[att_rows(2 * c + 1 - x, 0, 192)], g.at[att_rows(me, 0, 192)], r.at[pl.ds(384, 192)]
        if s == 2:
            return (g.at[att_rows(me, 2 * (1 - b0), 96)], g.at[att_rows(me, 2 * b0, 96)],
                    r.at[pl.ds(576, 96)])
        return (g.at[att_rows(me, 2 * b0 + 1 - b1, 48)], g.at[att_rows(me, 2 * b0 + b1, 48)],
                r.at[pl.ds(672, 48)])

    def kept(piece):
        if piece < FF_PIECES:
            return gff.at[piece, c, x, b0, b1], rx.at[piece], off_ref.at[piece]
        own = wdn.at[piece - FF_PIECES, att_rows(2 * c + x, 2 * b0 + b1, 48)]
        return own, rxa.at[piece - FF_PIECES], oat_ref.at[piece - FF_PIECES]

    def stage_copy(s, piece):
        sems = (gs.at[s, piece], gr.at[s, piece])
        order = ORDERS[piece]
        if s < 4:
            away, _, got = halves(piece, s)
            return send(away, got, *sems, core if s == 0 else peer[order[s - 1]])
        own, got, out = kept(piece)
        if s < 4 + n_exchange:
            return send(own, got.at[s - 4], *sems, dps[s - 2])
        back = [axis for axis in order if axis != "x"]
        if s == 4 + n_exchange:
            part = out.at[b0, b1]
            return send(part, part, *sems, peer[back[1]])
        part = out.at[b0] if back[0] == "y" else out.at[:, b1]
        return send(part, part, *sems, peer[back[0]])

    def combine(s, piece):
        if s < 4:
            _, keep, got = halves(piece, s)
            keep[...] = keep[...] + got[...]
        elif s < 4 + n_exchange:
            own, got, out = kept(piece)
            total = own[...] + got[s - 4]
            if s == 3 + n_exchange:
                out[b0, b1] = total
            else:
                own[...] = total

    def run_stage(s, piece):
        if s > 0:
            stage_copy(s - 1, piece).wait()
            combine(s - 1, piece)
        if s < last:
            stage_copy(s, piece).start()

    def late_stage(piece, s):
        if s < 5:
            run_stage(s, piece)
        elif s == 5:
            for k in range(5, 5 + n_exchange):
                run_stage(k, piece)
        else:
            run_stage(s + n_exchange - 1, piece)

    def down_grad(i, carry):
        def shard(s, carry):
            value = dot_tn(hid[s, :, block(i, 256)], glow[...]).astype(BF16)
            for q in range(4):
                gff[i, lax.rem(s, 2), s // 2, q // 2, q % 2] = value[64 * q:64 * (q + 1)]
            return carry

        lax.fori_loop(0, 4, shard, 0)
        for k in range(3):
            @pl.when(i == k)
            def _():
                run_stage(0, k)
                if k > 0:
                    run_stage(1, k - 1)

        return carry

    lax.fori_loop(0, 3, down_grad, 0)

    def ffn_back(s, carry):
        @pl.when(s == 1)
        def _():
            run_stage(1, 2)

        def rows(rb, carry):
            at = block(rb, 256)
            low = (dot_nt(glow[at], wdn[s]) * gd[s, at].astype(F32)).astype(BF16)
            gd[s, at] = low
            add_vec(8 + s, col_sum(low.astype(F32)))
            acc[at] = acc[at] + dot_nt(low, wup[s])
            return carry

        lax.fori_loop(0, 2, rows, 0)
        return carry

    lax.fori_loop(0, 4, ffn_back, 0)
    for device in partners:
        pl.semaphore_signal(free_sem, inc=1, device_id=device, device_id_type=MESH)

    def up_grad(i, carry):
        def shard(s, carry):
            value = dot_tn(flow[:, block(i, 256)], gd[s]).astype(BF16)
            for q in range(4):
                gff[3 + i, lax.rem(s, 2), s // 2, q // 2, q % 2] = value[64 * q:64 * (q + 1)]
            return carry

        lax.fori_loop(0, 4, shard, 0)
        for k in range(3):
            @pl.when(i == k)
            def _():
                run_stage(0, 3 + k)
                if k > 0:
                    run_stage(1, 2 + k)

        return carry

    lax.fori_loop(0, 3, up_grad, 0)

    def first_back(rb, carry):
        at = block(rb, 128)
        grad = gr2[at] + acc[at]
        normed = n1[at]
        add_vec(4, col_sum(grad * normed))
        add_vec(5, col_sum(grad))
        back = norm_back(grad * gain1, normed, r1[at])
        low = back.astype(BF16)
        acc[at] = back
        glow[at] = low
        add_vec(3, col_sum(low.astype(F32)))
        return carry

    lax.fori_loop(0, 4, first_back, 0)
    run_stage(1, 5)

    pl.semaphore_wait(free_sem, len(partners))

    def out_back(s, carry):
        home = att_rows(2 * lax.rem(s, 2) + s // 2, 0, 192)
        wdn[0, home] = dot_tn(ctx[s], glow[...]).astype(BF16)
        back = dot_nt(glow[...], wo[s]).astype(BF16)
        for j in range(3):
            gctx[3 * s + j] = back[:, 64 * j:64 * (j + 1)]
        return carry

    lax.fori_loop(0, 4, out_back, 0)
    run_stage(0, 6)

    def head_back(n, carry):
        s = slot_of(lax.rem(n, 4))
        j = n // 4
        h = 3 * s + j
        keys = qkv[h, :, 64:128]
        values = qkv[h, :, 128:192]
        keys_t = keys.T
        st[...] = jnp.zeros_like(st)

        def rows(rb, carry):
            at = block(rb, 512)
            query = qkv[h, at, 0:64]
            gout = gctx[h, at]
            lane = lax.broadcasted_iota(jnp.int32, (512, 128), 1)
            norm = jnp.sum(jnp.where(lane == j, lse[s, at], 0.0), -1, keepdims=True)
            probs = jnp.exp(dot_nt(query, keys) * 0.125 + key_mask - norm)
            gprobs = dot_nt(gout, values)
            scored = probs * (gprobs - jnp.sum(gprobs * probs, -1, keepdims=True))
            scored = scored.astype(BF16)
            st[0:64, at] = dot_nt(keys_t, scored)
            st[64:128] = st[64:128] + dot_tn(query, scored)
            st[128:192] = st[128:192] + dot_tn(gout, probs.astype(BF16))
            return carry

        lax.fori_loop(0, SEQ // 512, rows, 0, unroll=True)
        row = lax.broadcasted_iota(jnp.int32, (192, 1), 0)
        packed = (st[...] * jnp.where(row < 128, 0.125, 1.0)).astype(BF16)
        home = att_rows(2 * lax.rem(s, 2) + s // 2, 0, 192)
        wdn[1 + j, home] = dot_nn(packed, tok[...]).astype(BF16)
        sums = dot_nt(jnp.ones((8, SEQ), BF16), packed)
        vec[pl.ds(12 + h, 1), 0:192] = sums[0:1]
        w_rows = wqkv[s, block(j, 192)]

        acc[...] = acc[...] + dot_tn(packed, w_rows)

        for k in range(12):
            @pl.when(n == k)
            def _():
                if k % 4 == 0:
                    run_stage(1, 6 + k // 4)
                if k % 4 == 3:
                    run_stage(0, 7 + k // 4)
                for piece, s in AFTER_HEAD.get(k, ()):
                    late_stage(piece, s)

        return carry

    lax.fori_loop(0, 12, head_back, 0)
    def vec_copy(k):
        return send(vec_acc.at[k], vec_in.at[k], vs.at[k], vr.at[k], partners[k])

    def vec_step(k):
        if k > 0:
            vec_copy(k - 1).wait()
            total = vec_acc[k - 1] + vec_in[k - 1]
            if k == len(partners):
                vec_out[...] = total
                return
            vec_acc[k] = total
        vec_copy(k).start()

    vec_step(0)
    gtok[...] = acc[...].astype(BF16)
    run_stage(1, 9)
    vec_step(1)
    tok_copies = spread(1, gtok, grad_out)
    for copy in (*tok_copies[:3], lay_copies[1]):
        copy.start()
    for piece, s in AFTER_LAST:
        if piece == -3:
            for k in (s,) if s < 5 else range(5, len(partners) + 1):
                vec_step(k)
        elif piece < 0:
            copies = tok_copies if piece == -1 else lay_copies
            copies[1].wait()
            copies[3].start()
        else:
            late_stage(piece, s)
    for copies in (lay_copies, tok_copies):
        copies[0].wait()
        copies[2].wait()
        copies[3].wait()


def run_layer(dp, tokens, cotangent, key_lengths, slot_counts, shards, vectors):
    dp_bits = dp.bit_length() - 1
    n_exchange = dp_bits - 2
    stages = 4 + n_exchange + 2
    links = dp_bits + 2
    vmem = pl.BlockSpec(memory_space=pltpu.VMEM)
    smem = pl.BlockSpec(memory_space=pltpu.SMEM)
    hbm = pl.BlockSpec(memory_space=pltpu.HBM)
    dma = pltpu.SemaphoreType.DMA
    return pl.pallas_call(
        functools.partial(layer_kernel, dp_bits),
        out_shape=[
            jax.ShapeDtypeStruct((4, SEQ, D), BF16),
            jax.ShapeDtypeStruct((4, SEQ, D), BF16),
            jax.ShapeDtypeStruct((6, 2, 2, 64, D), BF16),
            jax.ShapeDtypeStruct((4, 2, 2, 48, D), BF16),
            jax.ShapeDtypeStruct((24, D), F32),
        ],
        in_specs=[hbm, hbm, smem, smem] + [hbm] * 4 + [vmem] * len(vectors),
        out_specs=[hbm] * 2 + [vmem] * 3,
        scratch_shapes=[
            *[pltpu.VMEM((4, *s.shape), BF16) for s in shards],
            pltpu.VMEM((4, 8, D), F32),
            pltpu.VMEM((SEQ, D), BF16),
            pltpu.VMEM((SEQ, D), BF16),
            pltpu.VMEM((12, SEQ, 192), BF16),
            pltpu.VMEM((4, SEQ, 192), BF16),
            pltpu.VMEM((4, SEQ, 128), F32),
            pltpu.VMEM((SEQ, D), F32),
            pltpu.VMEM((SEQ, 1), F32),
            pltpu.VMEM((SEQ, D), BF16),
            pltpu.VMEM((4, SEQ, D), BF16),
            pltpu.VMEM((4, SEQ, D), BF16),
            pltpu.VMEM((SEQ, D), F32),
            pltpu.VMEM((SEQ, D), BF16),
            pltpu.VMEM((SEQ, D), F32),
            pltpu.VMEM((12, SEQ, 64), BF16),
            pltpu.VMEM((192, SEQ), F32),
            pltpu.VMEM((2, SEQ, D), BF16),
            pltpu.VMEM((6, 2, 2, 2, 2, 64, D), BF16),
            pltpu.VMEM((6, 2, 2, 2, 64, D), BF16),
            pltpu.VMEM((6, 2, 2, 64, D), BF16),
            pltpu.VMEM((6, 2, 64, D), BF16),
            pltpu.VMEM((6, 64, D), BF16),
            pltpu.VMEM((6, n_exchange, 64, D), BF16),
            pltpu.VMEM((4, n_exchange, 48, D), BF16),
            pltpu.VMEM((links, 24, D), F32),
            pltpu.VMEM((links, 24, D), F32),
            dma((8, 5)), dma((8, 5)),
            dma((stages, PIECES)), dma((stages, PIECES)),
            dma((links,)), dma((links,)),
            dma((2, 3)), dma((2, 3)),
            dma((3,)), dma((3,)),
            dma((8,)),
            pltpu.SemaphoreType.REGULAR,
            pltpu.VMEM((16, D), F32),
        ],
        compiler_params=pltpu.CompilerParams(
            collective_id=0, has_side_effects=True, vmem_limit_bytes=67043328
        ),
    )(tokens, cotangent, key_lengths, slot_counts, *shards, *vectors)


def finish_kernel(layer, grad, ff, att, vec, layer_out, grad_out, down, up, out, g_q, g_k, g_v, *sums):
    layer_out[...] = layer[0]
    grad_out[...] = grad[0]
    down[...] = ff[0].astype(F32)
    up[...] = ff[1].astype(F32)

    @pl.when(pl.program_id(0) == 0)
    def _():
        t = lax.axis_index("tensor")
        out[...] = att[0].astype(F32)
        for i, ref in enumerate((g_q, g_k, g_v)):
            for j in range(3):
                ref[64 * j:64 * (j + 1)] = att[1 + j, 64 * i:64 * (i + 1)].astype(F32)
        for i, ref in enumerate(sums):
            row = vec[i:i + 1] if i < 6 else vec[pl.ds(8 + t, 1)]
            ref[...] = row.reshape(D)


def finish(layer, grad, ff, att, vec):
    rows, part = 4 * SEQ, ff.shape[1] // 4
    shard = jax.ShapeDtypeStruct(att.shape[1:], F32)
    square = jax.ShapeDtypeStruct(ff.shape[1:], F32)
    line = jax.ShapeDtypeStruct((D,), F32)
    slot_in = pl.BlockSpec((1, SEQ, D), lambda i: (i, 0, 0))
    slot_out = pl.BlockSpec((SEQ, D), lambda i: (i, 0))
    part_out = pl.BlockSpec((part, D), lambda i: (i, 0))
    return pl.pallas_call(
        finish_kernel,
        grid=(4,),
        out_shape=[jax.ShapeDtypeStruct((rows, D), BF16)] * 2 + [square] * 2 + [shard] * 4 + [line] * 7,
        in_specs=[slot_in, slot_in, pl.BlockSpec((2, part, D), lambda i: (0, i, 0)),
                  pl.BlockSpec(att.shape, lambda i: (0, 0, 0)), pl.BlockSpec(vec.shape, lambda i: (0, 0))],
        out_specs=[slot_out, slot_out, part_out, part_out]
        + [pl.BlockSpec(shard.shape, lambda i: (0, 0))] * 4
        + [pl.BlockSpec((D,), lambda i: (0,))] * 7,
        compiler_params=pltpu.CompilerParams(vmem_limit_bytes=67043328),
    )(layer, grad, ff, att, vec)


def per_device(dp, tokens, cotangent, key_lengths, slot_counts, *params):
    (w_query, b_query, w_key, w_value, b_value, w_out, b_out, attn_gain, attn_shift,
     w_up, b_up, w_down, b_down, ffn_gain, ffn_shift) = params
    slot = lax.axis_index("tensor")
    heads = w_query.shape[1] // HD
    qkv = jnp.stack([w.reshape(D, heads, HD) for w in (w_query, w_key, w_value)], 1)
    qkv = qkv.transpose(2, 1, 3, 0).reshape(-1, D)
    vectors = (b_out, attn_gain, attn_shift, b_down, ffn_gain, ffn_shift, b_up, b_query, b_value)
    layer, grad, off, oat, vec = run_layer(
        dp, tokens, cotangent, key_lengths, slot_counts, (qkv, w_out, w_up, w_down), vectors
    )
    layer, grad, g_down, g_up, g_out, g_q, g_k, g_v, *sums = finish(
        layer, grad, off.reshape(2, -1, D), oat.reshape(4, -1, D), vec
    )
    b_qkv = lax.dynamic_slice_in_dim(vec[12:, :3 * HD], slot * heads, heads)
    return (layer, grad, g_q.T, b_qkv[:, :HD].reshape(-1), g_k.T, g_v.T,
            b_qkv[:, 2 * HD:].reshape(-1), g_out, sums[3], sums[4], sums[5], g_up, sums[6],
            g_down, sums[0], sums[1], sums[2])


def solution(mesh):
    placed = (
        P("dp", None),
        P("dp", None),
        P("dp"),
        P("dp"),
        P(None, "tensor"),
        P("tensor"),
        P(None, "tensor"),
        P(None, "tensor"),
        P("tensor"),
        P("tensor", None),
        P(),
        P(),
        P(),
        P(None, "tensor"),
        P("tensor"),
        P("tensor", None),
        P(),
        P(),
        P(),
    )
    return jax.shard_map(
        functools.partial(per_device, mesh.shape["dp"]),
        mesh=mesh,
        in_specs=placed,
        out_specs=(
            P("dp", None),
            P("dp", None),
            P(None, "tensor"),
            P("tensor"),
            P(None, "tensor"),
            P(None, "tensor"),
            P("tensor"),
            P("tensor", None),
            P(),
            P(),
            P(),
            P(None, "tensor"),
            P("tensor"),
            P("tensor", None),
            P(),
            P(),
            P(),
        ),
        check_vma=False,
    )
```
